32 devices in a mesh: reg: 16 (over z, x, core), lev: 2 (over y).
Axes of the slice: x: 2, y: 2, z: 4, core: 2. Of those that a mesh axis runs over, the one named last changes fastest.
Arguments:
- state_now: bfloat16 [24, 1280, 2560], P(None, 'reg', 'lev'), may hold values from -6 to 6
- dep_cell: int32 [8, 1280, 2560], P(None, 'reg', 'lev'), may hold values from 0 to 63, as said below
- weight_code: int32 [8, 1280, 2560], P(None, 'reg', 'lev'), may hold values from 0 to 288, as said below
- wave_speed: float32 [8], replicated, may hold values from 0.05 to 5
Outputs:
- state_next: bfloat16 [24, 1280, 2560], P(None, 'reg', 'lev')
The draws below stay inside these ranges and needn't reach their ends.
Inputs may be any that keep to these rules, and one draw needn't show every extreme that they name: `dep_cell`: 2 * 4 (a + 4) + b + 4 with whole numbers a and b from -4 to 3; both ends of that range occur for a and for b. `weight_code`: 17 a + b with whole numbers a and b from 0 to 16.
All inputs are finite; a program needn't handle non-finite values.
Results may differ from the reference program's by a relative error of at most 0.0084.
Values may be sent and summed in bfloat16 or wider, within the bound.
A program may use at most 64 MiB of HBM per device.

```python
import math
import jax
import jax.numpy as jnp
from jax import lax

NLAT = 1280
NLON = 2560
MX = 640
MY = 640
LEVS = 8
FIELDS = 3
HALO = 4


def draw_dep_cell(key, part):
    key_rows, key_cols = jax.random.split(jax.random.fold_in(key, 11))
    shift_row = jax.random.randint(key_rows, (LEVS, NLAT, NLON), -HALO, HALO)
    shift_col = jax.random.randint(key_cols, (LEVS, NLAT, NLON), -HALO, HALO)
    shift_row = shift_row.at[0, 1, 1].set(-HALO).at[0, 2, 2].set(HALO - 1).at[0, 0, 0].set(-1).at[1, 0, 0].set(0)
    shift_col = shift_col.at[0, 1, 1].set(HALO - 1).at[0, 2, 2].set(-HALO).at[0, 0, 0].set(-1).at[1, 0, 0].set(0)
    shift_row = shift_row.at[0, 5, 5].set(HALO - 1).at[0, 6, 6].set(-HALO)
    shift_col = shift_col.at[0, 5, 5].set(HALO - 1).at[0, 6, 6].set(-HALO)
    return ((shift_row + HALO) * (2 * HALO) + (shift_col + HALO)).astype(jnp.int32)


def draw_weight_code(key, part):
    key_rows, key_cols = jax.random.split(jax.random.fold_in(key, 23))
    weight_row = jax.random.randint(key_rows, (LEVS, NLAT, NLON), 0, 17)
    weight_col = jax.random.randint(key_cols, (LEVS, NLAT, NLON), 0, 17)
    codes = 17 * weight_row + weight_col
    codes = codes.at[0, 3, 3].set(288).at[0, 4, 4].set(0)
    return codes.astype(jnp.int32)


def shard_levels(own_key, extent, cuts, low, top_value):
    factor_of, own = 1.0, jax.random.fold_in(own_key, 6)
    for dim, blocks in cuts:
        heights = jnp.exp(jax.random.uniform(jax.random.fold_in(own, dim), (blocks,), jnp.float32, low / len(cuts), top_value / len(cuts)))
        factor_of = factor_of * jnp.repeat(heights, extent[dim] // blocks).reshape([-1 if axis == dim else 1 for axis in range(len(extent))])
    return factor_of


def gaussian(own_key, shape, width, limit, cuts=(), held_as=jnp.bfloat16):
    result = width * jax.random.normal(own_key, shape, jnp.float32)
    if cuts:
        result = result * shard_levels(own_key, shape, cuts, -0.22, 0.18)
    return jnp.clip(result, -limit, limit).astype(held_as)


def setup_inputs(seed: int = 0) -> dict:
    keys = jax.random.split(jax.random.key(seed), 5)
    state_now = gaussian(keys[0], (FIELDS * LEVS, NLAT, NLON), 1.0, 6.0, ((1, 16), (2, 2)))
    dep_cell = draw_dep_cell(jax.random.fold_in(keys[4], 71), 0)
    weight_code = draw_weight_code(jax.random.fold_in(keys[4], 71), 0)
    wave_speed = jnp.clip(jnp.exp(jax.random.uniform(keys[3], (LEVS,), jnp.float32, math.log(0.05), math.log(5.0))), 0.05, 5.0)
    return dict(state_now=state_now, dep_cell=dep_cell, weight_code=weight_code, wave_speed=wave_speed)


def wave_table(length, modes, offset, amount):
    position = offset + lax.iota(jnp.int32, amount)
    wavenum = lax.iota(jnp.int32, 2 * modes) % modes
    product = (position[:, None] * wavenum[None, :]) % length
    angles = product.astype(jnp.float32) * (2.0 * math.pi / length)
    cosine_part = lax.iota(jnp.int32, 2 * modes) < modes
    return jnp.where(cosine_part[None, :], jnp.cos(angles), jnp.sin(angles)).astype(jnp.bfloat16)


def implicit_solve(spectral, xindex, speeds):
    wave_x = xindex % MX
    wave_y = lax.iota(jnp.int32, 2 * MY) % MY
    kx_term = (2.0 * math.pi / NLON) * wave_x.astype(jnp.float32)
    ky_term = (2.0 * math.pi / NLAT) * wave_y.astype(jnp.float32)
    laplace = kx_term[:, None] ** 2 + ky_term[None, :] ** 2
    inside = (wave_x[:, None] * wave_x[:, None] + wave_y[None, :] * wave_y[None, :] < MX * MY)
    weight_x = jnp.where(wave_x == 0, 1.0, 2.0)
    weight_y = jnp.where(wave_y == 0, 1.0, 2.0)
    factor = jnp.where(inside, weight_x[:, None] * weight_y[None, :], 0.0).astype(jnp.float32)
    speed_sq = speeds[:, None, None]
    vorticity = spectral[:, 0]
    divergence = spectral[:, 1]
    pressure = spectral[:, 2]
    div_new = (divergence + laplace * pressure) / (1.0 + speed_sq * laplace)
    pres_new = pressure - speed_sq * div_new
    stacked = jnp.stack([vorticity, div_new, pres_new], axis=1)
    return (stacked * factor[None, None]).astype(jnp.bfloat16)


def interpolate_level(inputs):
    field_data, cell_code, code_index = inputs
    flat_pos = lax.iota(jnp.int32, NLAT * NLON)
    row_arrive = flat_pos // NLON
    col_arrive = flat_pos % NLON
    shift_row = cell_code // (2 * HALO) - HALO
    shift_col = cell_code % (2 * HALO) - HALO
    row_index = (row_arrive + shift_row + NLAT) % NLAT
    col_index = (col_arrive + shift_col + NLON) % NLON
    row_next = (row_index + 1) % NLAT
    col_next = (col_index + 1) % NLON
    weight_row = (code_index // 17).astype(jnp.float32) / 16.0
    weight_col = (code_index % 17).astype(jnp.float32) / 16.0

    def sample(rows_at, cols_at):
        return field_data[:, rows_at * NLON + cols_at].astype(jnp.float32)

    blended = ((1.0 - weight_row) * (1.0 - weight_col) * sample(row_index, col_index)
               + (1.0 - weight_row) * weight_col * sample(row_index, col_next)
               + weight_row * (1.0 - weight_col) * sample(row_next, col_index)
               + weight_row * weight_col * sample(row_next, col_next))
    return blended.astype(jnp.bfloat16)


def reference(state_now, dep_cell, weight_code, wave_speed):
    stacked = FIELDS * LEVS
    upstream = lax.map(interpolate_level, (state_now.reshape(LEVS, FIELDS, NLAT * NLON),
                                           dep_cell.reshape(LEVS, NLAT * NLON),
                                           weight_code.reshape(LEVS, NLAT * NLON)))
    lon_table = wave_table(NLON, MX, 0, NLON)
    lat_table = wave_table(NLAT, MY, 0, NLAT)
    lon_sum = jnp.dot(upstream.reshape(stacked * NLAT, NLON), lon_table, preferred_element_type=jnp.float32)
    lon_coef = (lon_sum / NLON).astype(jnp.bfloat16).reshape(stacked, NLAT, 2 * MX)
    by_coef = lon_coef.transpose(0, 2, 1).reshape(stacked * 2 * MX, NLAT)
    spectral = jnp.dot(by_coef, lat_table, preferred_element_type=jnp.float32) / NLAT
    spectral = spectral.reshape(LEVS, FIELDS, 2 * MX, 2 * MY)
    solved = implicit_solve(spectral, lax.iota(jnp.int32, 2 * MX), wave_speed)
    back_lat = jnp.dot(solved.reshape(stacked * 2 * MX, 2 * MY), lat_table.T,
                       preferred_element_type=jnp.float32).astype(jnp.bfloat16)
    by_row = back_lat.reshape(stacked, 2 * MX, NLAT).transpose(0, 2, 1).reshape(stacked * NLAT, 2 * MX)
    state_next = jnp.dot(by_row, lon_table.T, preferred_element_type=jnp.float32).astype(jnp.bfloat16)
    return state_next.reshape(stacked, NLAT, NLON)
```

```python
import math

import jax
import jax.numpy as jnp
import ml_dtypes
import numpy as np
from jax import lax
from jax.experimental import pallas as pl
from jax.experimental.pallas import tpu as pltpu
from jax.sharding import PartitionSpec as P

NLAT = 1280
NLON = 2560
MX = 640
MY = 640
FIELDS = 3
HALO = 4
LANES = 128
ROWS = 16


def padded_2(block, sides, width):
    for axis, dim in sides:
        count = lax.axis_size(axis)
        forward = [(i, i + 1) for i in range(count - 1)]
        forward.append((count - 1, 0))
        backward = [(target, source) for source, target in forward]
        low = lax.ppermute(
            lax.slice_in_dim(block, block.shape[dim] - width, None, axis=dim), axis, forward
        )
        high = lax.ppermute(lax.slice_in_dim(block, 0, width, axis=dim), axis, backward)
        block = jnp.concatenate([low, block, high], axis=dim)
    return block


def wave_table(length, modes, offset, amount):
    position = offset + lax.iota(jnp.int32, amount)
    wavenum = lax.iota(jnp.int32, 2 * modes) % modes
    product = position[:, None] * wavenum[None, :] % length
    angles = product.astype(jnp.float32) * (2.0 * math.pi / length)
    cosine_part = lax.iota(jnp.int32, 2 * modes) < modes
    return jnp.where(cosine_part[None, :], jnp.cos(angles), jnp.sin(angles)).astype(jnp.bfloat16)


def implicit_solve(spectral, xindex, speeds):
    wave_x = xindex % MX
    wave_y = lax.iota(jnp.int32, 2 * MY) % MY
    kx_term = 2.0 * math.pi / NLON * wave_x.astype(jnp.float32)
    ky_term = 2.0 * math.pi / NLAT * wave_y.astype(jnp.float32)
    laplace = kx_term[:, None] ** 2 + ky_term[None, :] ** 2
    inside = wave_x[:, None] * wave_x[:, None] + wave_y[None, :] * wave_y[None, :] < MX * MY
    weight_x = jnp.where(wave_x == 0, 1.0, 2.0)
    weight_y = jnp.where(wave_y == 0, 1.0, 2.0)
    factor = jnp.where(inside, weight_x[:, None] * weight_y[None, :], 0.0).astype(jnp.float32)
    speed_sq = speeds[:, None, None]
    vorticity = spectral[:, 0]
    divergence = spectral[:, 1]
    pressure = spectral[:, 2]
    div_new = (divergence + laplace * pressure) / (1.0 + speed_sq * laplace)
    pres_new = pressure - speed_sq * div_new
    stacked = jnp.stack([vorticity, div_new, pres_new], axis=1)
    return (stacked * factor[None, None]).astype(jnp.bfloat16)


def shift_weights(cell_code, code_index):
    shift_row = cell_code // (2 * HALO) - HALO
    shift_col = cell_code % (2 * HALO) - HALO
    weight_row = (code_index // 17).astype(jnp.float32) / 16.0
    weight_col = (code_index % 17).astype(jnp.float32) / 16.0
    row_weights = []
    col_weights = []
    for offset in range(-HALO, HALO + 1):
        row_weights.append(
            jnp.where(shift_row == offset, 1.0 - weight_row, 0.0)
            + jnp.where(shift_row + 1 == offset, weight_row, 0.0)
        )
        col_weights.append(
            jnp.where(shift_col == offset, 1.0 - weight_col, 0.0)
            + jnp.where(shift_col + 1 == offset, weight_col, 0.0)
        )
    return (row_weights, col_weights)


def interpolate_local(padded, row_weights, col_weights):
    levels, rows_pad, cols_pad = padded.shape
    rows_here = rows_pad - 2 * HALO
    cols_here = cols_pad - 2 * HALO
    blended = jnp.zeros((levels, rows_here, cols_here), jnp.float32)
    for row_step in range(2 * HALO + 1):
        inner = jnp.zeros((levels, rows_here, cols_here), jnp.float32)
        for col_step in range(2 * HALO + 1):
            window = padded[:, row_step : row_step + rows_here, col_step : col_step + cols_here]
            inner = inner + col_weights[col_step] * window.astype(jnp.float32)
        blended = blended + row_weights[row_step] * inner
    return blended.astype(jnp.bfloat16)


def per_device(state_now, dep_cell, weight_code, wave_speed):
    stacked, rows_here, cols_here = state_now.shape
    levels = stacked // FIELDS
    col_first = lax.axis_index("lev") * cols_here
    grouped = state_now.reshape(levels, FIELDS, rows_here, cols_here)
    row_weights, col_weights = shift_weights(dep_cell, weight_code)
    passes = []
    for which_field in range(FIELDS):
        padded = padded_2(grouped[:, which_field], (("reg", 1), ("lev", 2)), HALO)
        passes.append(interpolate_local(padded, row_weights, col_weights))
    upstream = jnp.stack(passes, axis=1).reshape(stacked, rows_here, cols_here)
    lon_table = wave_table(NLON, MX, 0, NLON)
    full_rows = lax.all_to_all(upstream, "lev", split_axis=0, concat_axis=2, tiled=True)
    lon_sum = jnp.einsum("krj,jc->krc", full_rows, lon_table, preferred_element_type=jnp.float32)
    lon_coef = (lon_sum / NLON).astype(jnp.bfloat16)
    lat_table = wave_table(NLAT, MY, 0, NLAT)
    spectral = (
        jnp.einsum(
            "klc,ly->kcy",
            lax.all_to_all(lon_coef, "reg", split_axis=2, concat_axis=1, tiled=True),
            lat_table,
            preferred_element_type=jnp.float32,
        )
        / NLAT
    )
    share = spectral.shape[1]
    xindex = lax.axis_index("reg") * share + lax.iota(jnp.int32, share)
    level_count = spectral.shape[0] // FIELDS
    speeds = lax.dynamic_slice_in_dim(
        wave_speed, lax.axis_index("lev") * level_count, level_count, 0
    )
    solved = implicit_solve(spectral.reshape(level_count, FIELDS, share, 2 * MY), xindex, speeds)
    solved = solved.reshape(level_count * FIELDS, share, 2 * MY)
    back_lat = jnp.einsum(
        "kcy,ly->kcl", solved, lat_table, preferred_element_type=jnp.float32
    ).astype(jnp.bfloat16)
    back_coef = lax.all_to_all(back_lat, "reg", split_axis=2, concat_axis=1, tiled=True)
    own_table = wave_table(NLON, MX, col_first, cols_here)
    return jnp.einsum(
        "kcr,jc->krj",
        lax.all_gather(back_coef, "lev", axis=0, tiled=True),
        own_table,
        preferred_element_type=jnp.float32,
    ).astype(jnp.bfloat16)


def halo_parts(state):
    rows_here, cols_here = state.shape[1:]
    count = lax.axis_size("reg")
    forward = [(i, (i + 1) % count) for i in range(count)]
    backward = [(target, source) for source, target in forward]
    low = lax.ppermute(state[:, rows_here - HALO :], "reg", forward)
    high = lax.ppermute(state[:, :HALO], "reg", backward)
    edge = jnp.concatenate([low, high], axis=1)
    edge = jnp.pad(edge, ((0, 0), (0, ROWS - 2 * HALO), (0, 0)))
    tall = jnp.concatenate(
        [
            jnp.concatenate([part[:, :, :LANES], part[:, :, cols_here - LANES :]], axis=2)
            for part in (state, edge)
        ],
        axis=1,
    )
    lane = np.r_[0:HALO, 2 * LANES - HALO : 2 * LANES]
    pick = jnp.asarray((np.arange(2 * LANES)[:, None] == lane[None, :]), jnp.bfloat16)
    spot = np.r_[LANES : LANES + HALO, LANES - HALO : LANES]
    place = jnp.asarray((spot[:, None] == np.arange(2 * LANES)[None, :]), jnp.bfloat16)
    picked = jnp.einsum(
        "krl,le->ekr", tall, pick, preferred_element_type=jnp.float32
    ).astype(jnp.bfloat16)
    other = lax.ppermute(picked, "lev", [(0, 1), (1, 0)])
    pads = jnp.einsum(
        "ekr,el->krl", other, place, preferred_element_type=jnp.float32
    ).astype(jnp.bfloat16)
    levels = state.shape[0] // FIELDS
    return (
        edge.reshape(levels, FIELDS, ROWS, cols_here),
        pads.reshape(levels, FIELDS, rows_here + ROWS, 2 * LANES),
    )


LEVELS = 2
SUB = 8
QUARTERS = 5
MESH = pl.DeviceIdType.MESH


def host_waves(length, wavenums, amount):
    angles = (np.arange(amount)[:, None] * wavenums[None, :] % length) * (2.0 * np.pi / length)
    both = np.concatenate([np.cos(angles), np.sin(angles)], axis=1)
    return both.astype(np.float32).astype(ml_dtypes.bfloat16)


def mux_pair(parts, bits):
    for bit, step in zip(bits, (4, 2, 1)):
        parts = [jnp.where(bit, parts[i + step], parts[i]) for i in range(len(parts) - step)]
    return parts


def bit_masks(cell):
    masks = []
    for bit in (32.0, 16.0, 8.0, 4.0, 2.0, 1.0):
        mask = cell >= jnp.asarray(bit, cell.dtype)
        masks.append(mask)
        cell = jnp.where(mask, cell - jnp.asarray(bit, cell.dtype), cell)
    return masks


class Step:
    def __init__(self, ins, out, scratch):
        (self.x, self.edge, self.pads, self.dep, self.weight, self.speed, self.perm, self.perm_codes,
         self.lon_fwd, self.lon_back, self.lat_fwd, self.lat_back) = ins
        self.out = out
        (self.xbuf, self.dbuf, self.wbuf, self.codes, self.shift, self.up, self.yl, self.yr, self.zs, self.zr,
         self.solved, self.bs, self.br, self.yb, self.asm, self.ost, self.tf, self.tb, self.lf, self.lb,
         self.load_sem, self.table_sem, self.y_sem, self.z_sem, self.b_sem, self.yb_sem, self.own_sem, self.out_sem) = scratch
        self.reg, self.lev = lax.axis_index("reg"), lax.axis_index("lev")
        self.count = lax.axis_size("reg")
        self.rows = self.x.shape[1]
        self.cols = self.x.shape[2]
        self.chunks = self.dep.shape[0] // LEVELS
        self.sign = (1 - 2 * self.lev).astype(jnp.float32)

    def loads(self, q):
        slot = q % 2
        fields = LEVELS * FIELDS
        ks = pl.ds(q * fields, fields)
        vs = pl.ds(q * LEVELS, LEVELS)
        mid = pl.ds(LANES, self.cols)
        tall = self.rows + ROWS
        pairs = [
            (self.x.at[ks], self.xbuf.at[slot, :, pl.ds(0, self.rows), mid]),
            (self.edge.at[ks], self.xbuf.at[slot, :, pl.ds(self.rows, ROWS), mid]),
            (self.pads.at[ks, :, pl.ds(0, LANES)], self.xbuf.at[slot, :, :, pl.ds(0, LANES)]),
            (self.pads.at[ks, :, pl.ds(LANES, LANES)], self.xbuf.at[slot, :, :, pl.ds(LANES + self.cols, LANES)]),
            (self.dep.at[vs], self.dbuf.at[slot]),
            (self.weight.at[vs], self.wbuf.at[slot]),
        ]
        return [pltpu.make_async_copy(a, b, self.load_sem.at[slot, i]) for i, (a, b) in enumerate(pairs)]

    def tables(self):
        other = 1 - self.lev
        pairs = [
            (self.lon_fwd.at[other], self.tf.at[1]), (self.lon_fwd.at[self.lev], self.tf.at[0]),
            (self.lat_fwd, self.lf), (self.lat_back, self.lb),
            (self.lon_back.at[self.lev], self.tb.at[pl.ds(0, MX)]), (self.lon_back.at[other], self.tb.at[pl.ds(MX, MX)]),
        ]
        return [pltpu.make_async_copy(a, b, self.table_sem.at[i]) for i, (a, b) in enumerate(pairs)]

    def y_copy(self, q):
        return pltpu.make_async_remote_copy(
            src_ref=self.yl.at[q % 2], dst_ref=self.yr.at[q], send_sem=self.y_sem.at[0, q], recv_sem=self.y_sem.at[1, q],
            device_id=(self.reg, 1 - self.lev), device_id_type=MESH)

    def yb_copy(self, q):
        return pltpu.make_async_remote_copy(
            src_ref=self.br.at[q], dst_ref=self.yb.at[q], send_sem=self.yb_sem.at[0, q], recv_sem=self.yb_sem.at[1, q],
            device_id=(self.reg, 1 - self.lev), device_id_type=MESH)

    def block(self, index):
        return pl.ds(pl.multiple_of(index * self.rows, ROWS), self.rows)

    def spread_start(self, q, src, dst, sems, own):
        pltpu.make_async_copy(src.at[q % 2, self.block(self.reg)], dst.at[q, self.block(self.reg)], own.at[q]).start()

        @pl.loop(1, self.count)
        def _(i):
            peer = lax.rem(self.reg + i, self.count)
            pltpu.make_async_remote_copy(
                src_ref=src.at[q % 2, self.block(peer)], dst_ref=dst.at[q, self.block(self.reg)],
                send_sem=sems.at[0, q], recv_sem=sems.at[1, q],
                device_id=(peer, self.lev), device_id_type=MESH).start()

    def spread_wait(self, q, src, dst, sems, own):
        pltpu.make_async_copy(src.at[q % 2, self.block(self.reg)], dst.at[q, self.block(self.reg)], own.at[q]).wait()
        most = pl.ds(0, (self.count - 1) * self.rows)
        whole = pltpu.make_async_remote_copy(
            src_ref=src.at[q % 2, most], dst_ref=dst.at[q, most], send_sem=sems.at[0, q], recv_sem=sems.at[1, q],
            device_id=(self.reg, 1 - self.lev), device_id_type=MESH)
        whole.wait_send()
        whole.wait_recv()

    def out_copy(self, q):
        fields = LEVELS * FIELDS
        return pltpu.make_async_copy(self.ost.at[q % 2], self.out.at[pl.ds(q * fields, fields)], self.out_sem.at[q % 2])

    def decode(self, q):
        slot = q % 2
        rows = LEVELS * self.rows
        block = 2 * LANES

        @pl.loop(0, self.cols // block)
        def _(n):
            cols = pl.ds(pl.multiple_of(n * block, block), block)
            cell = self.dbuf[slot, :, :, cols].reshape(rows, block)
            both = self.wbuf[slot, :, :, cols].reshape(rows, block)
            high = (both * 241) >> 12
            for i, code in enumerate((cell, high, both - 17 * high)):
                code = code.astype(jnp.float32).astype(jnp.bfloat16)
                moved = jnp.dot(self.perm_codes[...], code, preferred_element_type=jnp.float32)
                self.codes[i, :, :, cols] = moved.astype(jnp.bfloat16).reshape(self.rows // SUB, ROWS, block)

    def spread_taps(self, q, piece):
        slot = q % 2
        width = self.shift.shape[4]
        taps = 2 * HALO + 1
        reach = self.shift.shape[2]
        part = reach // 2
        window = pl.ds(pl.multiple_of(piece * width, LANES), width + 2 * LANES)

        @pl.loop(0, FIELDS * 2)
        def _(n):
            field, half = n // 2, n % 2
            block = jnp.concatenate([self.xbuf[slot, field, :, window], self.xbuf[slot, FIELDS + field, :, window]], axis=0)
            perm = self.perm[pl.ds(pl.multiple_of(half * part * ROWS, ROWS), part * ROWS)]
            moved = jnp.dot(perm, block, preferred_element_type=jnp.float32)
            for tap in range(taps):
                turned = pltpu.roll(moved, (HALO - tap) % moved.shape[1], axis=1)[:, LANES : LANES + width]
                self.shift[field, tap, pl.ds(half * part, part)] = turned.astype(jnp.bfloat16).reshape(part, ROWS, width)

    def blend(self, q, piece):
        slot = q % 2
        width = self.shift.shape[4]
        taps = 2 * HALO + 1
        tiles = width // LANES

        @pl.loop(0, self.rows // SUB // 2 * tiles)
        def _(step):
            row = 2 * (step // tiles)
            col = pl.multiple_of(step % tiles * LANES, LANES)
            cols = pl.ds(col, LANES)
            all_cols = pl.ds(pl.multiple_of(piece * width + col, LANES), LANES)
            masks = [bit_masks(self.codes[0, row + sub, :, all_cols]) for sub in range(2)]
            weights = []
            for sub in range(2):
                high = self.codes[1, row + sub, :, all_cols].astype(jnp.float32) * (1.0 / 16.0)
                low = self.codes[2, row + sub, :, all_cols].astype(jnp.float32) * (1.0 / 16.0)
                weights.append((high, low))
            for field in range(FIELDS):
                near, far = [[], []], [[], []]
                for tap in range(taps):
                    parts = [self.shift[field, tap, row + i, :, cols] for i in range(taps + 1)]
                    for sub in range(2):
                        first, second = mux_pair(parts[sub : sub + taps], masks[sub][:3])
                        near[sub].append(first)
                        far[sub].append(second)
                for sub in range(2):
                    low = [part.astype(jnp.float32) for part in mux_pair(near[sub], masks[sub][3:])]
                    high = [part.astype(jnp.float32) for part in mux_pair(far[sub], masks[sub][3:])]
                    weight_row, weight_col = weights[sub]
                    upper = (1.0 - weight_col) * low[0] + weight_col * low[1]
                    lower = (1.0 - weight_col) * high[0] + weight_col * high[1]
                    value = (1.0 - weight_row) * upper + weight_row * lower
                    place = pl.ds(pl.multiple_of((row + sub) * ROWS, ROWS), ROWS)
                    self.up[slot, field, place, all_cols] = value.astype(jnp.bfloat16)

    def partial(self, q, field, table):
        total = jnp.dot(self.up[q % 2, field], self.tf[table], preferred_element_type=jnp.float32) * (1.0 / NLON)
        total = total.reshape(self.rows // SUB, LEVELS, SUB, total.shape[1])
        return [total[:, level].reshape(self.rows, total.shape[3]) for level in range(LEVELS)]

    def leave(self, q):
        @pl.loop(0, FIELDS)
        def _(field):
            for level, part in enumerate(self.partial(q, field, 1)):
                self.yl[q % 2, level, field] = part.astype(jnp.bfloat16)

        self.y_copy(q).start()

    def places(self, field):
        tiles = MX // LANES
        if field > 0:
            return [(tile, field - 1) for tile in range(tiles)]
        return [(tiles + tile // 2, tile % 2) for tile in range(tiles)]

    def join(self, q):
        self.y_copy(q).wait()
        roles = self.count // LEVELS
        for field in range(FIELDS):
            for level, part in enumerate(self.partial(q, field, 0)):
                whole = (part * self.sign + self.yr[q, level, field].astype(jnp.float32)).astype(jnp.bfloat16)
                for tile, (role, half) in enumerate(self.places(field)):
                    piece = whole[:, tile * LANES : (tile + 1) * LANES]
                    rows = pl.ds((level * roles + role) * self.rows, self.rows)
                    self.zs[q % 2, rows, half * LANES : (half + 1) * LANES] = piece
                    if field == 0 and tile == MX // LANES - 1:
                        self.zs[q % 2, rows, LANES:] = piece
        self.spread_start(q, self.zs, self.zr, self.z_sem, self.own_sem.at[0])

    def factor(self, wave_x, wave_y):
        inside = wave_x * wave_x + wave_y * wave_y < MX * MY
        weight = jnp.where(wave_x == 0, 1.0, 2.0) * jnp.where(wave_y == 0, 1.0, 2.0)
        return jnp.where(inside, weight, 0.0).astype(jnp.float32)

    def solve(self, q):
        self.spread_wait(q, self.zs, self.zr, self.z_sem, self.own_sem.at[0])
        roles = self.count // LEVELS
        tiles = MX // LANES
        role = lax.rem(self.reg, roles)
        coupled = role < tiles
        first = jnp.where(coupled, role, 2 * (role - tiles))
        second = jnp.where(coupled, role, jnp.minimum(2 * (role - tiles) + 1, tiles - 1))
        speed = self.speed[q * LEVELS + self.reg // roles]
        block = 2 * LANES
        gate = jnp.where(coupled, 1.0, 0.0)

        @pl.loop(0, self.lf.shape[0] // block)
        def _(n):
            rows = pl.ds(pl.multiple_of(n * block, block), block)
            spectral = jnp.dot(self.lf[rows], self.zr[q], preferred_element_type=jnp.float32) * (1.0 / NLAT)
            lane = lax.broadcasted_iota(jnp.int32, (block, LANES), 1)
            wave_y = lax.rem(lax.broadcasted_iota(jnp.int32, (block, LANES), 0) + n * block, MY)
            waves = [2 * lax.rem(lane + tile * LANES, MX // 2) + self.lev for tile in (first, second)]
            kx_term = 2.0 * math.pi / NLON * waves[0].astype(jnp.float32)
            ky_term = 2.0 * math.pi / NLAT * wave_y.astype(jnp.float32)
            laplace = kx_term * kx_term + ky_term * ky_term
            one, two = spectral[:, :LANES], spectral[:, LANES:]
            div_new = (one + laplace * two) / (1.0 + speed * laplace)
            pres_new = two - speed * div_new
            one = jnp.where(gate > 0.5, div_new, one) * self.factor(waves[0], wave_y)
            two = jnp.where(gate > 0.5, pres_new, two) * self.factor(waves[1], wave_y)
            self.solved[rows, :LANES] = one.astype(jnp.bfloat16)
            self.solved[rows, LANES:] = two.astype(jnp.bfloat16)

        @pl.loop(0, self.lb.shape[0] // block)
        def _(n):
            rows = pl.ds(pl.multiple_of(n * block, block), block)
            back = jnp.dot(self.lb[rows], self.solved[...], preferred_element_type=jnp.float32)
            self.bs[q % 2, rows] = back.astype(jnp.bfloat16)

        self.spread_start(q, self.bs, self.br, self.b_sem, self.own_sem.at[1])

    def cross(self, q):
        self.spread_wait(q, self.bs, self.br, self.b_sem, self.own_sem.at[1])
        self.yb_copy(q).start()

    def finish(self, q):
        self.yb_copy(q).wait()
        roles = self.count // LEVELS
        for level in range(LEVELS):
            for field in range(FIELDS):
                place = pl.ds((level * FIELDS + field) * self.rows, self.rows)
                for tile, (role, half) in enumerate(self.places(field)):
                    rows = pl.ds((level * roles + role) * self.rows, self.rows)
                    lanes = slice(half * LANES, (half + 1) * LANES)
                    mine = self.br[q, rows, lanes] * self.sign.astype(jnp.bfloat16)
                    self.asm[place, tile * LANES : (tile + 1) * LANES] = mine
                    self.asm[place, MX + tile * LANES : MX + (tile + 1) * LANES] = self.yb[q, rows, lanes]

        @pl.when(q >= 2)
        def _():
            self.out_copy(q - 2).wait()

        block = 2 * LANES

        @pl.loop(0, self.cols // block)
        def _(n):
            cols = pl.ds(pl.multiple_of(n * block, block), block)
            value = jnp.dot(self.asm[...], self.tb[:, cols], preferred_element_type=jnp.float32)
            self.ost[q % 2, :, :, cols] = value.astype(jnp.bfloat16).reshape(LEVELS * FIELDS, self.rows, block)

        self.out_copy(q).start()

    def run(self):
        barrier = pltpu.get_barrier_semaphore()

        @pl.loop(1, self.count)
        def _(i):
            peer = lax.rem(self.reg + i, self.count)
            pl.semaphore_signal(barrier, inc=1, device_id=(peer, self.lev), device_id_type=MESH)

        pl.semaphore_signal(barrier, inc=1, device_id=(self.reg, 1 - self.lev), device_id_type=MESH)
        for copy in self.loads(0):
            copy.start()
        for copy in self.tables():
            copy.start()
        pl.semaphore_wait(barrier, self.count)
        total = self.chunks
        pieces = self.cols // self.shift.shape[4]
        join_at, solve_at, cross_at, finish_at = OFFSETS

        def at(step, offset, stage):
            q = step - offset

            @pl.when((q >= 0) & (q < total))
            def _():
                stage(q)

        @pl.loop(0, total + finish_at)
        def _(step):
            @pl.when(step < total)
            def _():
                for copy in self.loads(step):
                    copy.wait()

                @pl.when(step + 1 < total)
                def _():
                    for copy in self.loads(step + 1):
                        copy.start()

                self.decode(step)
                for piece in range(pieces - 1):
                    self.spread_taps(step, piece)
                    self.blend(step, piece)

            @pl.when(step == 0)
            def _():
                for copy in self.tables():
                    copy.wait()

            at(step, join_at, self.join)
            at(step, solve_at, self.solve)

            @pl.when(step < total)
            def _():
                self.spread_taps(step, pieces - 1)
                self.blend(step, pieces - 1)
                self.leave(step)

            at(step, cross_at, self.cross)
            at(step, finish_at, self.finish)

        for q in range(total - 2, total):
            self.out_copy(q).wait()


OFFSETS = (1, 2, 3, 4)


def step_kernel(*refs):
    Step(refs[:12], refs[12], refs[13:]).run()


def row_source(rows, row):
    if row < 0:
        return rows + HALO + row
    if row >= rows:
        return HALO + row
    return row


def paired_device(state_now, dep_cell, weight_code, wave_speed):
    stacked, rows, cols = state_now.shape
    levels = stacked // FIELDS
    edge, pads = halo_parts(state_now)
    edge = edge.reshape(stacked, ROWS, cols)
    pads = pads.reshape(stacked, rows + ROWS, 2 * LANES)
    chunks = levels // LEVELS
    count = lax.axis_size("reg")
    run = rows // SUB
    reach = run + 2 * HALO
    tall = rows + ROWS
    perm = np.zeros((reach * ROWS, LEVELS * tall), np.float32)
    perm_codes = np.zeros((run * ROWS, LEVELS * rows), np.float32)
    for level in range(LEVELS):
        for sub in range(SUB):
            for near in range(reach):
                perm[near * ROWS + level * SUB + sub, level * tall + row_source(rows, run * sub + near - HALO)] = 1.0
            for near in range(run):
                perm_codes[near * ROWS + level * SUB + sub, level * rows + run * sub + near] = 1.0
    half = MX // 2
    waves = [host_waves(NLON, 2 * np.arange(half) + odd, cols) for odd in range(2)]
    lon_fwd = np.stack(waves)
    lat = host_waves(NLAT, np.arange(MY), NLAT)
    order = (np.arange(NLAT).reshape(count, SUB, run).transpose(0, 2, 1)).reshape(-1)
    bf16 = jnp.bfloat16
    consts = [jnp.asarray(a, bf16) for a in (perm, perm_codes)]
    consts += [jnp.asarray(np.ascontiguousarray(a)) for a in
               (lon_fwd, lon_fwd.transpose(0, 2, 1), lat[order].T, lat)]
    fields = LEVELS * FIELDS
    width = cols // 2
    taps = 2 * HALO + 1
    vm, dma = pltpu.VMEM, pltpu.SemaphoreType.DMA
    scratch = [
        vm((2, fields, tall, cols + 2 * LANES), bf16),
        vm((2, LEVELS, rows, cols), jnp.int32),
        vm((2, LEVELS, rows, cols), jnp.int32),
        vm((3, run, ROWS, cols), bf16),
        vm((FIELDS, taps, reach, ROWS, width), bf16),
        vm((2, FIELDS, run * ROWS, cols), bf16),
        vm((2, LEVELS, FIELDS, rows, MX), bf16),
        vm((chunks, LEVELS, FIELDS, rows, MX), bf16),
        vm((2, NLAT, 2 * LANES), bf16),
        vm((chunks, NLAT, 2 * LANES), bf16),
        vm((2 * MY, 2 * LANES), bf16),
        vm((2, NLAT, 2 * LANES), bf16),
        vm((chunks, NLAT, 2 * LANES), bf16),
        vm((chunks, NLAT, 2 * LANES), bf16),
        vm((fields * rows, 2 * MX), bf16),
        vm((2, fields, rows, cols), bf16),
        vm((2, cols, MX), bf16),
        vm((2 * MX, cols), bf16),
        vm((2 * MY, NLAT), bf16),
        vm((NLAT, 2 * MY), bf16),
        dma((2, 6)), dma((6,)), dma((2, chunks)), dma((2, chunks)), dma((2, chunks)), dma((2, chunks)),
        dma((2, chunks)), dma((2,)),
    ]
    hbm = pl.BlockSpec(memory_space=pl.ANY)
    vmem = pl.BlockSpec(memory_space=pltpu.VMEM)
    return pl.pallas_call(
        step_kernel,
        out_shape=jax.ShapeDtypeStruct((stacked, rows, cols), bf16),
        in_specs=[hbm] * 5 + [pl.BlockSpec(memory_space=pltpu.SMEM), vmem, vmem] + [hbm] * 4,
        out_specs=hbm,
        scratch_shapes=scratch,
        compiler_params=pltpu.CompilerParams(vmem_limit_bytes=60 << 20, collective_id=0, has_side_effects=True),
        cost_estimate=pl.CostEstimate(flops=20 * 10**9, bytes_accessed=40 * 10**6, transcendentals=0),
        name="step",
    )(state_now, edge, pads, dep_cell, weight_code, wave_speed, *consts)


def solution(mesh):
    placed = (P(None, "reg", "lev"), P(None, "reg", "lev"), P(None, "reg", "lev"), P())
    paired = mesh.shape["lev"] == 2 and mesh.shape["reg"] == 16
    return jax.shard_map(
        paired_device if paired else per_device,
        mesh=mesh,
        in_specs=placed,
        out_specs=P(None, "reg", "lev"),
        check_vma=False,
    )
```

```python
import math

import jax
import jax.numpy as jnp
import ml_dtypes
import numpy as np
from jax import lax
from jax.experimental import pallas as pl
from jax.experimental.pallas import tpu as pltpu
from jax.sharding import PartitionSpec as P

NLAT = 1280
NLON = 2560
MX = 640
MY = 640
FIELDS = 3
HALO = 4
LANES = 128
ROWS = 16


def padded_2(block, sides, width):
    for axis, dim in sides:
        count = lax.axis_size(axis)
        forward = [(i, i + 1) for i in range(count - 1)]
        forward.append((count - 1, 0))
        backward = [(target, source) for source, target in forward]
        low = lax.ppermute(
            lax.slice_in_dim(block, block.shape[dim] - width, None, axis=dim), axis, forward
        )
        high = lax.ppermute(lax.slice_in_dim(block, 0, width, axis=dim), axis, backward)
        block = jnp.concatenate([low, block, high], axis=dim)
    return block


def wave_table(length, modes, offset, amount):
    position = offset + lax.iota(jnp.int32, amount)
    wavenum = lax.iota(jnp.int32, 2 * modes) % modes
    product = position[:, None] * wavenum[None, :] % length
    angles = product.astype(jnp.float32) * (2.0 * math.pi / length)
    cosine_part = lax.iota(jnp.int32, 2 * modes) < modes
    return jnp.where(cosine_part[None, :], jnp.cos(angles), jnp.sin(angles)).astype(jnp.bfloat16)


def implicit_solve(spectral, xindex, speeds):
    wave_x = xindex % MX
    wave_y = lax.iota(jnp.int32, 2 * MY) % MY
    kx_term = 2.0 * math.pi / NLON * wave_x.astype(jnp.float32)
    ky_term = 2.0 * math.pi / NLAT * wave_y.astype(jnp.float32)
    laplace = kx_term[:, None] ** 2 + ky_term[None, :] ** 2
    inside = wave_x[:, None] * wave_x[:, None] + wave_y[None, :] * wave_y[None, :] < MX * MY
    weight_x = jnp.where(wave_x == 0, 1.0, 2.0)
    weight_y = jnp.where(wave_y == 0, 1.0, 2.0)
    factor = jnp.where(inside, weight_x[:, None] * weight_y[None, :], 0.0).astype(jnp.float32)
    speed_sq = speeds[:, None, None]
    vorticity = spectral[:, 0]
    divergence = spectral[:, 1]
    pressure = spectral[:, 2]
    div_new = (divergence + laplace * pressure) / (1.0 + speed_sq * laplace)
    pres_new = pressure - speed_sq * div_new
    stacked = jnp.stack([vorticity, div_new, pres_new], axis=1)
    return (stacked * factor[None, None]).astype(jnp.bfloat16)


def shift_weights(cell_code, code_index):
    shift_row = cell_code // (2 * HALO) - HALO
    shift_col = cell_code % (2 * HALO) - HALO
    weight_row = (code_index // 17).astype(jnp.float32) / 16.0
    weight_col = (code_index % 17).astype(jnp.float32) / 16.0
    row_weights = []
    col_weights = []
    for offset in range(-HALO, HALO + 1):
        row_weights.append(
            jnp.where(shift_row == offset, 1.0 - weight_row, 0.0)
            + jnp.where(shift_row + 1 == offset, weight_row, 0.0)
        )
        col_weights.append(
            jnp.where(shift_col == offset, 1.0 - weight_col, 0.0)
            + jnp.where(shift_col + 1 == offset, weight_col, 0.0)
        )
    return (row_weights, col_weights)


def interpolate_local(padded, row_weights, col_weights):
    levels, rows_pad, cols_pad = padded.shape
    rows_here = rows_pad - 2 * HALO
    cols_here = cols_pad - 2 * HALO
    blended = jnp.zeros((levels, rows_here, cols_here), jnp.float32)
    for row_step in range(2 * HALO + 1):
        inner = jnp.zeros((levels, rows_here, cols_here), jnp.float32)
        for col_step in range(2 * HALO + 1):
            window = padded[:, row_step : row_step + rows_here, col_step : col_step + cols_here]
            inner = inner + col_weights[col_step] * window.astype(jnp.float32)
        blended = blended + row_weights[row_step] * inner
    return blended.astype(jnp.bfloat16)


def per_device(state_now, dep_cell, weight_code, wave_speed):
    stacked, rows_here, cols_here = state_now.shape
    levels = stacked // FIELDS
    col_first = lax.axis_index("lev") * cols_here
    grouped = state_now.reshape(levels, FIELDS, rows_here, cols_here)
    row_weights, col_weights = shift_weights(dep_cell, weight_code)
    passes = []
    for which_field in range(FIELDS):
        padded = padded_2(grouped[:, which_field], (("reg", 1), ("lev", 2)), HALO)
        passes.append(interpolate_local(padded, row_weights, col_weights))
    upstream = jnp.stack(passes, axis=1).reshape(stacked, rows_here, cols_here)
    lon_table = wave_table(NLON, MX, 0, NLON)
    full_rows = lax.all_to_all(upstream, "lev", split_axis=0, concat_axis=2, tiled=True)
    lon_sum = jnp.einsum("krj,jc->krc", full_rows, lon_table, preferred_element_type=jnp.float32)
    lon_coef = (lon_sum / NLON).astype(jnp.bfloat16)
    lat_table = wave_table(NLAT, MY, 0, NLAT)
    spectral = (
        jnp.einsum(
            "klc,ly->kcy",
            lax.all_to_all(lon_coef, "reg", split_axis=2, concat_axis=1, tiled=True),
            lat_table,
            preferred_element_type=jnp.float32,
        )
        / NLAT
    )
    share = spectral.shape[1]
    xindex = lax.axis_index("reg") * share + lax.iota(jnp.int32, share)
    level_count = spectral.shape[0] // FIELDS
    speeds = lax.dynamic_slice_in_dim(
        wave_speed, lax.axis_index("lev") * level_count, level_count, 0
    )
    solved = implicit_solve(spectral.reshape(level_count, FIELDS, share, 2 * MY), xindex, speeds)
    solved = solved.reshape(level_count * FIELDS, share, 2 * MY)
    back_lat = jnp.einsum(
        "kcy,ly->kcl", solved, lat_table, preferred_element_type=jnp.float32
    ).astype(jnp.bfloat16)
    back_coef = lax.all_to_all(back_lat, "reg", split_axis=2, concat_axis=1, tiled=True)
    own_table = wave_table(NLON, MX, col_first, cols_here)
    return jnp.einsum(
        "kcr,jc->krj",
        lax.all_gather(back_coef, "lev", axis=0, tiled=True),
        own_table,
        preferred_element_type=jnp.float32,
    ).astype(jnp.bfloat16)


def halo_parts(state):
    rows_here, cols_here = state.shape[1:]
    count = lax.axis_size("reg")
    forward = [(i, (i + 1) % count) for i in range(count)]
    backward = [(target, source) for source, target in forward]
    low = lax.ppermute(state[:, rows_here - HALO :], "reg", forward)
    high = lax.ppermute(state[:, :HALO], "reg", backward)
    edge = jnp.concatenate([low, high], axis=1)
    edge = jnp.pad(edge, ((0, 0), (0, ROWS - 2 * HALO), (0, 0)))
    tall = jnp.concatenate(
        [
            jnp.concatenate([part[:, :, :LANES], part[:, :, cols_here - LANES :]], axis=2)
            for part in (state, edge)
        ],
        axis=1,
    )
    lane = np.r_[0:HALO, 2 * LANES - HALO : 2 * LANES]
    pick = jnp.asarray((np.arange(2 * LANES)[:, None] == lane[None, :]), jnp.bfloat16)
    spot = np.r_[LANES : LANES + HALO, LANES - HALO : LANES]
    place = jnp.asarray((spot[:, None] == np.arange(2 * LANES)[None, :]), jnp.bfloat16)
    picked = jnp.einsum(
        "krl,le->ekr", tall, pick, preferred_element_type=jnp.float32
    ).astype(jnp.bfloat16)
    other = lax.ppermute(picked, "lev", [(0, 1), (1, 0)])
    pads = jnp.einsum(
        "ekr,el->krl", other, place, preferred_element_type=jnp.float32
    ).astype(jnp.bfloat16)
    levels = state.shape[0] // FIELDS
    return (
        edge.reshape(levels, FIELDS, ROWS, cols_here),
        pads.reshape(levels, FIELDS, rows_here + ROWS, 2 * LANES),
    )


LEVELS = 2
SUB = 8
GROUP = 4
MESH = pl.DeviceIdType.MESH


def host_waves(length, wavenums, amount):
    angles = (np.arange(amount)[:, None] * wavenums[None, :] % length) * (2.0 * np.pi / length)
    both = np.concatenate([np.cos(angles), np.sin(angles)], axis=1)
    return both.astype(np.float32).astype(ml_dtypes.bfloat16)


def mux_pair(parts, bits):
    for bit, step in zip(bits, (4, 2, 1)):
        parts = [jnp.where(bit, parts[i + step], parts[i]) for i in range(len(parts) - step)]
    return parts


def bit_masks(cell):
    masks = []
    for bit in (32.0, 16.0, 8.0, 4.0, 2.0, 1.0):
        mask = cell >= jnp.asarray(bit, cell.dtype)
        masks.append(mask)
        cell = jnp.where(mask, cell - jnp.asarray(bit, cell.dtype), cell)
    return masks


class Step:
    def __init__(self, ins, out, scratch):
        (self.x, self.edge, self.pads, self.dep, self.weight, self.speed, self.perm, self.perm_codes,
         self.lon_fwd, self.lon_back, self.lat_fwd, self.lat_back) = ins
        self.out = out
        (self.xbuf, self.dbuf, self.wbuf, self.codes, self.shift, self.up, self.yl, self.yr, self.zs, self.zr,
         self.solved, self.bs, self.br, self.yb, self.asm, self.ost, self.tf, self.tb, self.lf, self.lb,
         self.load_sem, self.table_sem, self.y_sem, self.z_sem, self.b_sem, self.bg_sem, self.yb_sem, self.own_sem, self.out_sem) = scratch
        self.reg, self.lev = lax.axis_index("reg"), lax.axis_index("lev")
        self.count = lax.axis_size("reg")
        self.rows = self.x.shape[1]
        self.group_rows = GROUP * self.rows
        self.cols = self.x.shape[2]
        self.chunks = self.dep.shape[0] // LEVELS
        self.sign = (1 - 2 * self.lev).astype(jnp.float32)

    def loads(self, q):
        fields = LEVELS * FIELDS
        ks = pl.ds(q * fields, fields)
        vs = pl.ds(q * LEVELS, LEVELS)
        mid = pl.ds(LANES, self.cols)
        tall = self.rows + ROWS
        pairs = [
            (self.x.at[ks], self.xbuf.at[:, pl.ds(0, self.rows), mid]),
            (self.edge.at[ks], self.xbuf.at[:, pl.ds(self.rows, ROWS), mid]),
            (self.pads.at[ks, :, pl.ds(0, LANES)], self.xbuf.at[:, :, pl.ds(0, LANES)]),
            (self.pads.at[ks, :, pl.ds(LANES, LANES)], self.xbuf.at[:, :, pl.ds(LANES + self.cols, LANES)]),
            (self.dep.at[vs], self.dbuf),
            (self.weight.at[vs], self.wbuf),
        ]
        return [pltpu.make_async_copy(a, b, self.load_sem.at[i]) for i, (a, b) in enumerate(pairs)]

    def tables(self):
        other = 1 - self.lev
        pairs = [
            (self.lon_fwd.at[other], self.tf.at[1]), (self.lon_fwd.at[self.lev], self.tf.at[0]),
            (self.lat_fwd, self.lf), (self.lat_back, self.lb),
            (self.lon_back.at[self.lev], self.tb.at[pl.ds(0, MX)]), (self.lon_back.at[other], self.tb.at[pl.ds(MX, MX)]),
        ]
        return [pltpu.make_async_copy(a, b, self.table_sem.at[i]) for i, (a, b) in enumerate(pairs)]

    def y_copy(self, q, field):
        return pltpu.make_async_remote_copy(
            src_ref=self.yl.at[q % 2, field], dst_ref=self.yr.at[q, field],
            send_sem=self.y_sem.at[0, q, field], recv_sem=self.y_sem.at[1, q, field],
            device_id=(self.reg, 1 - self.lev), device_id_type=MESH)

    def yb_copy(self, q, group):
        rows = pl.ds(pl.multiple_of(group * self.group_rows, ROWS), self.group_rows)
        return pltpu.make_async_remote_copy(
            src_ref=self.br.at[q, rows], dst_ref=self.yb.at[q, rows],
            send_sem=self.yb_sem.at[0, q, group], recv_sem=self.yb_sem.at[1, q, group],
            device_id=(self.reg, 1 - self.lev), device_id_type=MESH)

    def block(self, index):
        return pl.ds(pl.multiple_of(index * self.rows, ROWS), self.rows)

    def to_peer(self, q, src, dst, send, recv, peer):
        return pltpu.make_async_remote_copy(
            src_ref=src.at[q % 2, self.block(peer)], dst_ref=dst.at[q, self.block(self.reg)],
            send_sem=send, recv_sem=recv, device_id=(peer, self.lev), device_id_type=MESH)

    def of_bytes(self, ref, rows, send, recv):
        part = ref.at[0, pl.ds(0, rows)]
        return pltpu.make_async_remote_copy(
            src_ref=part, dst_ref=part, send_sem=send, recv_sem=recv,
            device_id=(self.reg, 1 - self.lev), device_id_type=MESH)

    def keep(self, q, src, dst, sem):
        return pltpu.make_async_copy(src.at[q % 2, self.block(self.reg)], dst.at[q, self.block(self.reg)], sem)

    def out_copy(self, q):
        fields = LEVELS * FIELDS
        return pltpu.make_async_copy(self.ost, self.out.at[pl.ds(q * fields, fields)], self.out_sem.at[0])

    def decode(self):
        rows = LEVELS * self.rows
        block = 2 * LANES

        @pl.loop(0, self.cols // block)
        def _(n):
            cols = pl.ds(pl.multiple_of(n * block, block), block)
            cell = self.dbuf[:, :, cols].reshape(rows, block)
            both = self.wbuf[:, :, cols].reshape(rows, block)
            high = (both * 241) >> 12
            for i, code in enumerate((cell, high, both - 17 * high)):
                code = code.astype(jnp.float32).astype(jnp.bfloat16)
                moved = jnp.dot(self.perm_codes[...], code, preferred_element_type=jnp.float32)
                self.codes[i, :, :, cols] = moved.astype(jnp.bfloat16).reshape(self.rows // SUB, ROWS, block)

    def spread_taps(self):
        width = self.cols
        taps = 2 * HALO + 1
        part = self.shift.shape[2] // 2

        @pl.loop(0, FIELDS * 2)
        def _(n):
            field, half = n // 2, n % 2
            block = jnp.concatenate([self.xbuf[field], self.xbuf[FIELDS + field]], axis=0)
            perm = self.perm[pl.ds(pl.multiple_of(half * part * ROWS, ROWS), part * ROWS)]
            moved = jnp.dot(perm, block, preferred_element_type=jnp.float32)
            for tap in range(taps):
                turned = pltpu.roll(moved, (HALO - tap) % moved.shape[1], axis=1)[:, LANES : LANES + width]
                self.shift[field, tap, pl.ds(half * part, part)] = turned.astype(jnp.bfloat16).reshape(part, ROWS, width)

    def blend(self, q, first, last):
        slot = q % 2
        taps = 2 * HALO + 1
        tile = 2 * LANES
        tiles = self.cols // tile

        @pl.loop(first * tiles, last * tiles)
        def _(step):
            row = 2 * (step // tiles)
            cols = pl.ds(pl.multiple_of(step % tiles * tile, tile), tile)
            masks = [bit_masks(self.codes[0, row + sub, :, cols]) for sub in range(2)]
            weights = []
            for sub in range(2):
                high = self.codes[1, row + sub, :, cols].astype(jnp.float32) * (1.0 / 16.0)
                low = self.codes[2, row + sub, :, cols].astype(jnp.float32) * (1.0 / 16.0)
                weights.append((high, low))
            for field in range(FIELDS):
                near, far = [[], []], [[], []]
                for tap in range(taps):
                    parts = [self.shift[field, tap, row + i, :, cols] for i in range(taps + 1)]
                    for sub in range(2):
                        first, second = mux_pair(parts[sub : sub + taps], masks[sub][:3])
                        near[sub].append(first)
                        far[sub].append(second)
                for sub in range(2):
                    low = [part.astype(jnp.float32) for part in mux_pair(near[sub], masks[sub][3:])]
                    high = [part.astype(jnp.float32) for part in mux_pair(far[sub], masks[sub][3:])]
                    weight_row, weight_col = weights[sub]
                    upper = (1.0 - weight_col) * low[0] + weight_col * low[1]
                    lower = (1.0 - weight_col) * high[0] + weight_col * high[1]
                    value = (1.0 - weight_row) * upper + weight_row * lower
                    place = pl.ds(pl.multiple_of((row + sub) * ROWS, ROWS), ROWS)
                    self.up[slot, field, place, cols] = value.astype(jnp.bfloat16)

    def partial(self, q, field, table):
        total = jnp.dot(self.up[q % 2, field], self.tf[table], preferred_element_type=jnp.float32) * (1.0 / NLON)
        total = total.reshape(self.rows // SUB, LEVELS, SUB, total.shape[1])
        return [total[:, level].reshape(self.rows, total.shape[3]) for level in range(LEVELS)]

    def leave(self, q):
        @pl.loop(0, FIELDS)
        def _(field):
            for level, part in enumerate(self.partial(q, field, 1)):
                self.yl[q % 2, field, level] = part.astype(jnp.bfloat16)
            self.y_copy(q, field).start()

    def places(self, field):
        tiles = MX // LANES
        if field > 0:
            return [(tile, field - 1) for tile in range(tiles)]
        return [(tiles + tile // 2, tile % 2) for tile in range(tiles)]

    def join(self, q):
        roles = self.count // LEVELS
        tiles = MX // LANES
        for field in range(FIELDS):
            self.y_copy(q, field).wait()
            for level, part in enumerate(self.partial(q, field, 0)):
                whole = (part * self.sign + self.yr[q, field, level].astype(jnp.float32)).astype(jnp.bfloat16)
                for tile, (role, half) in enumerate(self.places(field)):
                    piece = whole[:, tile * LANES : (tile + 1) * LANES]
                    rows = pl.ds((level * roles + role) * self.rows, self.rows)
                    self.zs[q % 2, rows, half * LANES : (half + 1) * LANES] = piece
                    if field == 0 and tile == tiles - 1:
                        self.zs[q % 2, rows, LANES:] = piece
            if field == 1:
                continue
            low, high = (tiles, roles) if field == 0 else (0, tiles)

            def wanted(device):
                role = lax.rem(device, roles)
                return (role >= low) & (role < high)

            @pl.loop(1, self.count)
            def _(i):
                peer = lax.bitwise_xor(self.reg, i)

                @pl.when(wanted(peer))
                def _():
                    self.to_peer(q, self.zs, self.zr, self.z_sem.at[0, q], self.z_sem.at[1, q], peer).start()

            @pl.when(wanted(self.reg))
            def _():
                self.keep(q, self.zs, self.zr, self.own_sem.at[0, q]).start()

    def factor(self, wave_x, wave_y):
        inside = wave_x * wave_x + wave_y * wave_y < MX * MY
        weight = jnp.where(wave_x == 0, 1.0, 2.0) * jnp.where(wave_y == 0, 1.0, 2.0)
        return jnp.where(inside, weight, 0.0).astype(jnp.float32)

    def solve(self, q):
        self.keep(q, self.zs, self.zr, self.own_sem.at[0, q]).wait()
        all_rows = self.of_bytes(self.zr, (self.count - 1) * self.rows, self.z_sem.at[0, q], self.z_sem.at[1, q])
        all_rows.wait_send()
        all_rows.wait_recv()
        roles = self.count // LEVELS
        tiles = MX // LANES
        role = lax.rem(self.reg, roles)
        coupled = role < tiles
        first = jnp.where(coupled, role, 2 * (role - tiles))
        second = jnp.where(coupled, role, jnp.minimum(2 * (role - tiles) + 1, tiles - 1))
        speed = self.speed[q * LEVELS + self.reg // roles]
        block = 2 * LANES
        gate = jnp.where(coupled, 1.0, 0.0)

        @pl.loop(0, self.lf.shape[0] // block)
        def _(n):
            rows = pl.ds(pl.multiple_of(n * block, block), block)
            spectral = jnp.dot(self.lf[rows], self.zr[q], preferred_element_type=jnp.float32) * (1.0 / NLAT)
            lane = lax.broadcasted_iota(jnp.int32, (block, LANES), 1)
            wave_y = lax.rem(lax.broadcasted_iota(jnp.int32, (block, LANES), 0) + n * block, MY)
            waves = [2 * lax.rem(lane + tile * LANES, MX // 2) + self.lev for tile in (first, second)]
            kx_term = 2.0 * math.pi / NLON * waves[0].astype(jnp.float32)
            ky_term = 2.0 * math.pi / NLAT * wave_y.astype(jnp.float32)
            laplace = kx_term * kx_term + ky_term * ky_term
            one, two = spectral[:, :LANES], spectral[:, LANES:]
            div_new = (one + laplace * two) / (1.0 + speed * laplace)
            pres_new = two - speed * div_new
            one = jnp.where(gate > 0.5, div_new, one) * self.factor(waves[0], wave_y)
            two = jnp.where(gate > 0.5, pres_new, two) * self.factor(waves[1], wave_y)
            self.solved[rows, :LANES] = one.astype(jnp.bfloat16)
            self.solved[rows, LANES:] = two.astype(jnp.bfloat16)

        @pl.loop(0, self.lb.shape[0] // block)
        def _(n):
            rows = pl.ds(pl.multiple_of(n * block, block), block)
            back = jnp.dot(self.lb[rows], self.solved[...], preferred_element_type=jnp.float32)
            self.bs[q % 2, rows] = back.astype(jnp.bfloat16)

        self.keep(q, self.bs, self.br, self.own_sem.at[1, q]).start()

        @pl.loop(1, self.count)
        def _(i):
            peer = lax.bitwise_xor(self.reg, i)
            self.to_peer(q, self.bs, self.br, self.b_sem.at[q], self.bg_sem.at[q, self.reg // GROUP], peer).start()

    def cross(self, q):
        mine = self.reg // GROUP
        self.keep(q, self.bs, self.br, self.own_sem.at[1, q]).wait()
        self.of_bytes(self.br, (GROUP - 1) * self.rows, self.b_sem.at[q], self.bg_sem.at[q, mine]).wait_recv()
        self.yb_copy(q, mine).start()

        @pl.loop(1, self.count // GROUP)
        def _(i):
            group = lax.bitwise_xor(mine, i)
            self.of_bytes(self.br, GROUP * self.rows, self.b_sem.at[q], self.bg_sem.at[q, group]).wait_recv()
            self.yb_copy(q, group).start()

        self.of_bytes(self.br, (self.count - 1) * self.rows, self.b_sem.at[q], self.bg_sem.at[q, mine]).wait_send()

    def finish(self, q):
        for group in range(self.count // GROUP):
            self.yb_copy(q, group).wait()
        roles = self.count // LEVELS
        for level in range(LEVELS):
            for field in range(FIELDS):
                place = pl.ds((level * FIELDS + field) * self.rows, self.rows)
                for tile, (role, half) in enumerate(self.places(field)):
                    rows = pl.ds((level * roles + role) * self.rows, self.rows)
                    lanes = slice(half * LANES, (half + 1) * LANES)
                    mine = self.br[q, rows, lanes] * self.sign.astype(jnp.bfloat16)
                    self.asm[place, tile * LANES : (tile + 1) * LANES] = mine
                    self.asm[place, MX + tile * LANES : MX + (tile + 1) * LANES] = self.yb[q, rows, lanes]

        @pl.when(q >= 1)
        def _():
            self.out_copy(q - 1).wait()

        block = 2 * LANES

        @pl.loop(0, self.cols // block)
        def _(n):
            cols = pl.ds(pl.multiple_of(n * block, block), block)
            value = jnp.dot(self.asm[...], self.tb[:, cols], preferred_element_type=jnp.float32)
            self.ost[:, :, cols] = value.astype(jnp.bfloat16).reshape(LEVELS * FIELDS, self.rows, block)

        self.out_copy(q).start()

    def run(self):
        barrier = pltpu.get_barrier_semaphore()

        @pl.loop(1, self.count)
        def _(i):
            peer = lax.rem(self.reg + i, self.count)
            pl.semaphore_signal(barrier, inc=1, device_id=(peer, self.lev), device_id_type=MESH)

        pl.semaphore_signal(barrier, inc=1, device_id=(self.reg, 1 - self.lev), device_id_type=MESH)
        for copy in self.loads(0):
            copy.start()
        total = self.chunks
        cut = 3
        end = self.rows // SUB // 2

        def at(step, offset, stage):
            q = step - offset

            @pl.when((q >= 0) & (q < total))
            def _():
                stage(q)

        @pl.loop(0, total + 4)
        def _(step):
            @pl.when(step < total)
            def _():
                for copy in self.loads(step):
                    copy.wait()

                @pl.when(step == 0)
                def _():
                    for copy in self.tables():
                        copy.start()

                self.decode()
                self.spread_taps()

                @pl.when(step == 0)
                def _():
                    pl.semaphore_wait(barrier, self.count)
                    for copy in self.tables():
                        copy.wait()

                @pl.when(step + 1 < total)
                def _():
                    for copy in self.loads(step + 1):
                        copy.start()

            at(step, 4, self.finish)
            at(step, 3, self.cross)
            at(step, 2, self.solve)

            @pl.when(step < total)
            def _():
                self.blend(step, 0, cut)

            at(step, 1, self.join)

            @pl.when(step < total)
            def _():
                self.blend(step, cut, end)

                self.leave(step)

        self.out_copy(total - 1).wait()


def step_kernel(*refs):
    Step(refs[:12], refs[12], refs[13:]).run()


def row_source(rows, row):
    if row < 0:
        return rows + HALO + row
    if row >= rows:
        return HALO + row
    return row


def paired_device(state_now, dep_cell, weight_code, wave_speed):
    stacked, rows, cols = state_now.shape
    levels = stacked // FIELDS
    edge, pads = halo_parts(state_now)
    edge = edge.reshape(stacked, ROWS, cols)
    pads = pads.reshape(stacked, rows + ROWS, 2 * LANES)
    chunks = levels // LEVELS
    count = lax.axis_size("reg")
    run = rows // SUB
    reach = run + 2 * HALO
    tall = rows + ROWS
    perm = np.zeros((reach * ROWS, LEVELS * tall), np.float32)
    perm_codes = np.zeros((run * ROWS, LEVELS * rows), np.float32)
    for level in range(LEVELS):
        for sub in range(SUB):
            for near in range(reach):
                perm[near * ROWS + level * SUB + sub, level * tall + row_source(rows, run * sub + near - HALO)] = 1.0
            for near in range(run):
                perm_codes[near * ROWS + level * SUB + sub, level * rows + run * sub + near] = 1.0
    half = MX // 2
    waves = [host_waves(NLON, 2 * np.arange(half) + odd, cols) for odd in range(2)]
    lon_fwd = np.stack(waves)
    lat = host_waves(NLAT, np.arange(MY), NLAT)
    order = (np.arange(NLAT).reshape(count, SUB, run).transpose(0, 2, 1)).reshape(-1)
    bf16 = jnp.bfloat16
    consts = [jnp.asarray(a, bf16) for a in (perm, perm_codes)]
    consts += [jnp.asarray(np.ascontiguousarray(a)) for a in
               (lon_fwd, lon_fwd.transpose(0, 2, 1), lat[order].T, lat)]
    fields = LEVELS * FIELDS
    groups = count // GROUP
    taps = 2 * HALO + 1
    vm, dma = pltpu.VMEM, pltpu.SemaphoreType.DMA
    scratch = [
        vm((fields, tall, cols + 2 * LANES), bf16),
        vm((LEVELS, rows, cols), jnp.int32),
        vm((LEVELS, rows, cols), jnp.int32),
        vm((3, run, ROWS, cols), bf16),
        vm((FIELDS, taps, reach, ROWS, cols), bf16),
        vm((2, FIELDS, run * ROWS, cols), bf16),
        vm((2, FIELDS, LEVELS, rows, MX), bf16),
        vm((chunks, FIELDS, LEVELS, rows, MX), bf16),
        vm((2, NLAT, 2 * LANES), bf16),
        vm((chunks, NLAT, 2 * LANES), bf16),
        vm((2 * MY, 2 * LANES), bf16),
        vm((2, NLAT, 2 * LANES), bf16),
        vm((chunks, NLAT, 2 * LANES), bf16),
        vm((chunks, NLAT, 2 * LANES), bf16),
        vm((fields * rows, 2 * MX), bf16),
        vm((fields, rows, cols), bf16),
        vm((2, cols, MX), bf16),
        vm((2 * MX, cols), bf16),
        vm((2 * MY, NLAT), bf16),
        vm((NLAT, 2 * MY), bf16),
        dma((6,)), dma((6,)), dma((2, chunks, FIELDS)), dma((2, chunks)), dma((chunks,)), dma((chunks, groups)),
        dma((2, chunks, groups)), dma((2, chunks)), dma((1,)),
    ]
    hbm = pl.BlockSpec(memory_space=pl.ANY)
    vmem = pl.BlockSpec(memory_space=pltpu.VMEM)
    return pl.pallas_call(
        step_kernel,
        out_shape=jax.ShapeDtypeStruct((stacked, rows, cols), bf16),
        in_specs=[hbm] * 5 + [pl.BlockSpec(memory_space=pltpu.SMEM), vmem, vmem] + [hbm] * 4,
        out_specs=hbm,
        scratch_shapes=scratch,
        compiler_params=pltpu.CompilerParams(vmem_limit_bytes=60 << 20, collective_id=0, has_side_effects=True),
        cost_estimate=pl.CostEstimate(flops=20 * 10**9, bytes_accessed=40 * 10**6, transcendentals=0),
        name="step",
    )(state_now, edge, pads, dep_cell, weight_code, wave_speed, *consts)


def solution(mesh):
    placed = (P(None, "reg", "lev"), P(None, "reg", "lev"), P(None, "reg", "lev"), P())
    paired = mesh.shape["lev"] == 2 and mesh.shape["reg"] == 16
    return jax.shard_map(
        paired_device if paired else per_device,
        mesh=mesh,
        in_specs=placed,
        out_specs=P(None, "reg", "lev"),
        check_vma=False,
    )
```

```python
import math

import jax
import jax.numpy as jnp
import ml_dtypes
import numpy as np
from jax import lax
from jax.experimental import pallas as pl
from jax.experimental.pallas import tpu as pltpu
from jax.sharding import PartitionSpec as P

NLAT = 1280
NLON = 2560
MX = 640
MY = 640
FIELDS = 3
HALO = 4
LANES = 128
ROWS = 16


def padded_2(block, sides, width):
    for axis, dim in sides:
        count = lax.axis_size(axis)
        forward = [(i, i + 1) for i in range(count - 1)]
        forward.append((count - 1, 0))
        backward = [(target, source) for source, target in forward]
        low = lax.ppermute(
            lax.slice_in_dim(block, block.shape[dim] - width, None, axis=dim), axis, forward
        )
        high = lax.ppermute(lax.slice_in_dim(block, 0, width, axis=dim), axis, backward)
        block = jnp.concatenate([low, block, high], axis=dim)
    return block


def wave_table(length, modes, offset, amount):
    position = offset + lax.iota(jnp.int32, amount)
    wavenum = lax.iota(jnp.int32, 2 * modes) % modes
    product = position[:, None] * wavenum[None, :] % length
    angles = product.astype(jnp.float32) * (2.0 * math.pi / length)
    cosine_part = lax.iota(jnp.int32, 2 * modes) < modes
    return jnp.where(cosine_part[None, :], jnp.cos(angles), jnp.sin(angles)).astype(jnp.bfloat16)


def implicit_solve(spectral, xindex, speeds):
    wave_x = xindex % MX
    wave_y = lax.iota(jnp.int32, 2 * MY) % MY
    kx_term = 2.0 * math.pi / NLON * wave_x.astype(jnp.float32)
    ky_term = 2.0 * math.pi / NLAT * wave_y.astype(jnp.float32)
    laplace = kx_term[:, None] ** 2 + ky_term[None, :] ** 2
    inside = wave_x[:, None] * wave_x[:, None] + wave_y[None, :] * wave_y[None, :] < MX * MY
    weight_x = jnp.where(wave_x == 0, 1.0, 2.0)
    weight_y = jnp.where(wave_y == 0, 1.0, 2.0)
    factor = jnp.where(inside, weight_x[:, None] * weight_y[None, :], 0.0).astype(jnp.float32)
    speed_sq = speeds[:, None, None]
    vorticity = spectral[:, 0]
    divergence = spectral[:, 1]
    pressure = spectral[:, 2]
    div_new = (divergence + laplace * pressure) / (1.0 + speed_sq * laplace)
    pres_new = pressure - speed_sq * div_new
    stacked = jnp.stack([vorticity, div_new, pres_new], axis=1)
    return (stacked * factor[None, None]).astype(jnp.bfloat16)


def shift_weights(cell_code, code_index):
    shift_row = cell_code // (2 * HALO) - HALO
    shift_col = cell_code % (2 * HALO) - HALO
    weight_row = (code_index // 17).astype(jnp.float32) / 16.0
    weight_col = (code_index % 17).astype(jnp.float32) / 16.0
    row_weights = []
    col_weights = []
    for offset in range(-HALO, HALO + 1):
        row_weights.append(
            jnp.where(shift_row == offset, 1.0 - weight_row, 0.0)
            + jnp.where(shift_row + 1 == offset, weight_row, 0.0)
        )
        col_weights.append(
            jnp.where(shift_col == offset, 1.0 - weight_col, 0.0)
            + jnp.where(shift_col + 1 == offset, weight_col, 0.0)
        )
    return (row_weights, col_weights)


def interpolate_local(padded, row_weights, col_weights):
    levels, rows_pad, cols_pad = padded.shape
    rows_here = rows_pad - 2 * HALO
    cols_here = cols_pad - 2 * HALO
    blended = jnp.zeros((levels, rows_here, cols_here), jnp.float32)
    for row_step in range(2 * HALO + 1):
        inner = jnp.zeros((levels, rows_here, cols_here), jnp.float32)
        for col_step in range(2 * HALO + 1):
            window = padded[:, row_step : row_step + rows_here, col_step : col_step + cols_here]
            inner = inner + col_weights[col_step] * window.astype(jnp.float32)
        blended = blended + row_weights[row_step] * inner
    return blended.astype(jnp.bfloat16)


def per_device(state_now, dep_cell, weight_code, wave_speed):
    stacked, rows_here, cols_here = state_now.shape
    levels = stacked // FIELDS
    col_first = lax.axis_index("lev") * cols_here
    grouped = state_now.reshape(levels, FIELDS, rows_here, cols_here)
    row_weights, col_weights = shift_weights(dep_cell, weight_code)
    passes = []
    for which_field in range(FIELDS):
        padded = padded_2(grouped[:, which_field], (("reg", 1), ("lev", 2)), HALO)
        passes.append(interpolate_local(padded, row_weights, col_weights))
    upstream = jnp.stack(passes, axis=1).reshape(stacked, rows_here, cols_here)
    lon_table = wave_table(NLON, MX, 0, NLON)
    full_rows = lax.all_to_all(upstream, "lev", split_axis=0, concat_axis=2, tiled=True)
    lon_sum = jnp.einsum("krj,jc->krc", full_rows, lon_table, preferred_element_type=jnp.float32)
    lon_coef = (lon_sum / NLON).astype(jnp.bfloat16)
    lat_table = wave_table(NLAT, MY, 0, NLAT)
    spectral = (
        jnp.einsum(
            "klc,ly->kcy",
            lax.all_to_all(lon_coef, "reg", split_axis=2, concat_axis=1, tiled=True),
            lat_table,
            preferred_element_type=jnp.float32,
        )
        / NLAT
    )
    share = spectral.shape[1]
    xindex = lax.axis_index("reg") * share + lax.iota(jnp.int32, share)
    level_count = spectral.shape[0] // FIELDS
    speeds = lax.dynamic_slice_in_dim(
        wave_speed, lax.axis_index("lev") * level_count, level_count, 0
    )
    solved = implicit_solve(spectral.reshape(level_count, FIELDS, share, 2 * MY), xindex, speeds)
    solved = solved.reshape(level_count * FIELDS, share, 2 * MY)
    back_lat = jnp.einsum(
        "kcy,ly->kcl", solved, lat_table, preferred_element_type=jnp.float32
    ).astype(jnp.bfloat16)
    back_coef = lax.all_to_all(back_lat, "reg", split_axis=2, concat_axis=1, tiled=True)
    own_table = wave_table(NLON, MX, col_first, cols_here)
    return jnp.einsum(
        "kcr,jc->krj",
        lax.all_gather(back_coef, "lev", axis=0, tiled=True),
        own_table,
        preferred_element_type=jnp.float32,
    ).astype(jnp.bfloat16)


LEVELS = 2
SUB = 8
MESH = pl.DeviceIdType.MESH


def host_waves(length, wavenums, amount):
    angles = (np.arange(amount)[:, None] * wavenums[None, :] % length) * (2.0 * np.pi / length)
    both = np.concatenate([np.cos(angles), np.sin(angles)], axis=1)
    return both.astype(np.float32).astype(ml_dtypes.bfloat16)


def mux_pair(parts, bits):
    for bit, step in zip(bits, (4, 2, 1)):
        parts = [jnp.where(bit, parts[i + step], parts[i]) for i in range(len(parts) - step)]
    return parts


def bit_masks(cell):
    masks = []
    for bit in (32.0, 16.0, 8.0, 4.0, 2.0, 1.0):
        mask = cell >= jnp.asarray(bit, cell.dtype)
        masks.append(mask)
        cell = jnp.where(mask, cell - jnp.asarray(bit, cell.dtype), cell)
    return masks


class Step:
    def __init__(self, ins, out, scratch):
        (self.x, self.dep, self.weight, self.speed, self.perm, self.perm_codes, self.pick,
         self.lon_fwd, self.lon_back, self.lat_fwd, self.lat_back) = ins
        self.out = out
        (self.xbuf, self.hrow, self.hedge, self.srow, self.sedge, self.scorner, self.dbuf, self.wbuf, self.codes, self.shift, self.up, self.yl, self.yr, self.zs, self.zr,
         self.waves, self.solved, self.bs, self.br, self.yb, self.asm, self.ost, self.tf, self.tb, self.lf, self.lb,
         self.load_sem, self.halo_sem, self.table_sem, self.y_sem, self.z_sem, self.b_sem, self.bg_sem, self.yb_sem, self.own_sem, self.out_sem) = scratch
        self.reg, self.lev = lax.axis_index("reg"), lax.axis_index("lev")
        self.count = lax.axis_size("reg")
        self.rows = self.x.shape[1]
        self.roles = self.count // LEVELS
        self.last = lax.rem(self.reg, self.roles) == self.roles - 1
        self.cols = self.x.shape[2]
        self.chunks = self.dep.shape[0] // LEVELS
        self.sign = (1 - 2 * self.lev).astype(jnp.float32)

    def loads(self, q, which=slice(None)):
        fields = LEVELS * FIELDS
        ks = pl.ds(q * fields, fields)
        vs = pl.ds(q * LEVELS, LEVELS)
        mid = pl.ds(LANES, self.cols)
        pairs = [
            (self.x.at[ks], self.xbuf.at[:, :, mid]),
            (self.dep.at[vs], self.dbuf),
            (self.weight.at[vs], self.wbuf),
        ]
        return [pltpu.make_async_copy(a, b, self.load_sem.at[i]) for i, (a, b) in list(enumerate(pairs))[which]]

    def halos(self, q):
        slot = q % 2
        up = lax.rem(self.reg + self.count - 1, self.count)
        down = lax.rem(self.reg + 1, self.count)
        other = 1 - self.lev
        mid = pl.ds(LANES, self.cols)
        left, right = pl.ds(0, LANES), pl.ds(LANES + self.cols, LANES)
        moves = [(self.sedge.at[slot], self.hedge.at[q], self.reg, other)]
        for side, to in enumerate((down, up)):
            moves.append((self.srow.at[slot, side], self.hrow.at[q, side, :, mid], to, self.lev))
            for lanes in (left, right):
                moves.append((self.scorner.at[slot, side], self.hrow.at[q, side, :, lanes], to, other))
        return [
            pltpu.make_async_remote_copy(
                src_ref=src, dst_ref=dst, send_sem=self.halo_sem.at[0, q, n], recv_sem=self.halo_sem.at[1, q, n],
                device_id=(reg, lev), device_id_type=MESH)
            for n, (src, dst, reg, lev) in enumerate(moves)
        ]

    def pack(self, q):
        slot = q % 2
        fields = LEVELS * FIELDS
        last = self.cols
        lane = lax.broadcasted_iota(jnp.int32, (1, LANES), 1)
        near = lane < LANES // 2
        edge = jnp.zeros((self.rows, LANES), jnp.float32)
        for k in range(fields):
            first = self.xbuf[k, :, LANES : 2 * LANES].astype(jnp.float32)
            final = self.xbuf[k, :, last : last + LANES].astype(jnp.float32)
            both = jnp.where(near, first, final)
            shift = 2 * HALO * k
            here = lax.rem(lane + (HALO + LANES - shift), LANES) < 2 * HALO
            edge = jnp.where(here, pltpu.roll(both, shift, axis=1) if shift else both, edge)
        self.sedge[slot] = edge.astype(jnp.bfloat16)
        for side, start in enumerate((self.rows - ROWS, 0)):
            slab = self.xbuf[:, start : start + ROWS, LANES : LANES + last].reshape(fields * ROWS, last)
            rows = jnp.dot(self.pick[side], slab, preferred_element_type=jnp.float32)
            self.srow[slot, side] = rows.astype(jnp.bfloat16)
            self.scorner[slot, side] = jnp.where(near, rows[:, :LANES], rows[:, last - LANES :]).astype(jnp.bfloat16)

    def unpack(self, q):
        edge = self.hedge[q].astype(jnp.float32)
        for k in range(LEVELS * FIELDS):
            tile = pltpu.roll(edge, LANES - 2 * HALO * k, axis=1) if k else edge
            tile = tile.astype(jnp.bfloat16)
            self.xbuf[k, :, :LANES] = tile
            self.xbuf[k, :, LANES + self.cols :] = tile

    def tables(self):
        other = 1 - self.lev
        pairs = [
            (self.lon_fwd.at[other], self.tf.at[1]), (self.lon_fwd.at[self.lev], self.tf.at[0]),
            (self.lat_fwd, self.lf), (self.lat_back, self.lb),
            (self.lon_back.at[self.lev], self.tb.at[pl.ds(0, MX)]), (self.lon_back.at[other], self.tb.at[pl.ds(MX, MX)]),
        ]
        return [pltpu.make_async_copy(a, b, self.table_sem.at[i]) for i, (a, b) in enumerate(pairs)]

    def y_copy(self, q, field):
        return pltpu.make_async_remote_copy(
            src_ref=self.yl.at[q % 2, field], dst_ref=self.yr.at[q, field],
            send_sem=self.y_sem.at[0, q, field], recv_sem=self.y_sem.at[1, q, field],
            device_id=(self.reg, 1 - self.lev), device_id_type=MESH)

    def yb_copies(self, q, level):
        full = self.count // LEVELS * self.rows
        near = (self.count // LEVELS // 2) * self.rows
        start = level * full
        parts = [
            (pl.ds(start, near), slice(None)),
            (pl.ds(start + near, full - near - self.rows), slice(None)),
            (pl.ds(start + full - self.rows, self.rows), pl.ds(0, LANES)),
        ]
        return [
            pltpu.make_async_remote_copy(
                src_ref=self.br.at[q, rows, lanes], dst_ref=self.yb.at[q, rows, lanes],
                send_sem=self.yb_sem.at[0, q, 3 * level + n], recv_sem=self.yb_sem.at[1, q, 3 * level + n],
                device_id=(self.reg, 1 - self.lev), device_id_type=MESH)
            for n, (rows, lanes) in enumerate(parts)
        ]

    def block(self, index):
        return pl.ds(pl.multiple_of(index * self.rows, ROWS), self.rows)

    def to_peer(self, q, src, dst, send, recv, peer, half=False):
        lanes = pl.ds(0, LANES) if half else slice(None)
        return pltpu.make_async_remote_copy(
            src_ref=src.at[q % 2, self.block(peer), lanes], dst_ref=dst.at[q, self.block(self.reg), lanes],
            send_sem=send, recv_sem=recv, device_id=(peer, self.lev), device_id_type=MESH)

    def of_bytes(self, ref, blocks, sem, half=False):
        lanes = pl.ds(0, LANES) if half else slice(None)
        part = ref.at[0, pl.ds(0, blocks * self.rows), lanes]
        return pltpu.make_async_copy(part, part, sem)

    def keep(self, q, src, dst, sem, half=False):
        lanes = pl.ds(0, LANES) if half else slice(None)
        return pltpu.make_async_copy(
            src.at[q % 2, self.block(self.reg), lanes], dst.at[q, self.block(self.reg), lanes], sem)

    def out_copy(self, q):
        fields = LEVELS * FIELDS
        return pltpu.make_async_copy(self.ost, self.out.at[pl.ds(q * fields, fields)], self.out_sem.at[0])

    def decode(self):
        rows = LEVELS * self.rows
        block = 2 * LANES

        @pl.loop(0, self.cols // block)
        def _(n):
            cols = pl.ds(pl.multiple_of(n * block, block), block)
            cell = self.dbuf[:, :, cols].reshape(rows, block)
            both = self.wbuf[:, :, cols].reshape(rows, block)
            high = (both * 241) >> 12
            for i, code in enumerate((cell, high, both - 17 * high)):
                code = code.astype(jnp.float32).astype(jnp.bfloat16)
                moved = jnp.dot(self.perm_codes[...], code, preferred_element_type=jnp.float32)
                self.codes[i, :, :, cols] = moved.astype(jnp.bfloat16).reshape(self.rows // SUB, ROWS, block)

    def spread_taps(self, q, field):
        width = self.cols
        taps = 2 * HALO + 1
        part = self.shift.shape[1] // 2

        @pl.loop(0, 2)
        def _(half):
            parts = [self.xbuf[field], self.xbuf[FIELDS + field], self.hrow[q, 0], self.hrow[q, 1]]
            block = jnp.concatenate(parts, axis=0)
            perm = self.perm[field, pl.ds(pl.multiple_of(half * part * ROWS, ROWS), part * ROWS)]
            moved = jnp.dot(perm, block, preferred_element_type=jnp.float32)
            for tap in range(taps):
                turned = pltpu.roll(moved, (HALO - tap) % moved.shape[1], axis=1)[:, LANES : LANES + width]
                self.shift[tap, pl.ds(half * part, part)] = turned.astype(jnp.bfloat16).reshape(part, ROWS, width)

    def blend(self, q, field):
        slot = q % 2
        taps = 2 * HALO + 1
        tile = 2 * LANES
        tiles = self.cols // tile

        @pl.loop(0, self.rows // SUB // 2 * tiles)
        def _(step):
            row = 2 * (step // tiles)
            cols = pl.ds(pl.multiple_of(step % tiles * tile, tile), tile)
            masks = [bit_masks(self.codes[0, row + sub, :, cols]) for sub in range(2)]
            near, far = [[], []], [[], []]
            for tap in range(taps):
                parts = [self.shift[tap, row + i, :, cols] for i in range(taps + 1)]
                for sub in range(2):
                    first, second = mux_pair(parts[sub : sub + taps], masks[sub][:3])
                    near[sub].append(first)
                    far[sub].append(second)
            for sub in range(2):
                low = [part.astype(jnp.float32) for part in mux_pair(near[sub], masks[sub][3:])]
                high = [part.astype(jnp.float32) for part in mux_pair(far[sub], masks[sub][3:])]
                weight_row = self.codes[1, row + sub, :, cols].astype(jnp.float32) * (1.0 / 16.0)
                weight_col = self.codes[2, row + sub, :, cols].astype(jnp.float32) * (1.0 / 16.0)
                upper = (1.0 - weight_col) * low[0] + weight_col * low[1]
                lower = (1.0 - weight_col) * high[0] + weight_col * high[1]
                value = (1.0 - weight_row) * upper + weight_row * lower
                place = pl.ds(pl.multiple_of((row + sub) * ROWS, ROWS), ROWS)
                self.up[slot, field, place, cols] = value.astype(jnp.bfloat16)

    def partial(self, q, field, table):
        total = jnp.dot(self.up[q % 2, field], self.tf[table], preferred_element_type=jnp.float32) * (1.0 / NLON)
        total = total.reshape(self.rows // SUB, LEVELS, SUB, total.shape[1])
        return [total[:, level].reshape(self.rows, total.shape[3]) for level in range(LEVELS)]

    def leave(self, q, field):
        for level, part in enumerate(self.partial(q, field, 1)):
            self.yl[q % 2, field, level] = part.astype(jnp.bfloat16)
        self.y_copy(q, field).start()

    def places(self, field):
        tiles = MX // LANES
        if field > 0:
            return [(tile, field - 1) for tile in range(tiles)]
        return [(tiles + tile // 2, tile % 2) for tile in range(tiles)]

    def join(self, q, field):
        roles = self.roles
        tiles = MX // LANES
        self.y_copy(q, field).wait()
        for level, part in enumerate(self.partial(q, field, 0)):
            whole = (part * self.sign + self.yr[q, field, level].astype(jnp.float32)).astype(jnp.bfloat16)
            for tile, (role, half) in enumerate(self.places(field)):
                rows = pl.ds((level * roles + role) * self.rows, self.rows)
                piece = whole[:, tile * LANES : (tile + 1) * LANES]
                self.zs[q % 2, rows, half * LANES : (half + 1) * LANES] = piece
        if field == 1:
            return
        full_sem, half_sem, recv_sem = self.z_sem.at[0, q], self.z_sem.at[1, q], self.z_sem.at[2, q]
        spread = roles - tiles if field == 0 else tiles
        for other in range(LEVELS):
            level = lax.rem(self.reg // roles + other, LEVELS)
            for turn in range(spread):
                role = tiles + turn if field == 0 else lax.rem(self.reg + turn, tiles)
                half = field == 0 and turn == spread - 1
                peer = level * roles + role
                send_sem = half_sem if half else full_sem

                @pl.when(peer != self.reg)
                def _():
                    self.to_peer(q, self.zs, self.zr, send_sem, recv_sem, peer, half).start()

                @pl.when(peer == self.reg)
                def _():
                    self.keep(q, self.zs, self.zr, self.own_sem.at[0, q], half).start()

    def arrive(self, q):
        others = self.count - 1

        @pl.when(self.last)
        def _():
            self.keep(q, self.zs, self.zr, self.own_sem.at[0, q], True).wait()
            self.of_bytes(self.zr, others, self.z_sem.at[2, q], True).wait()
            self.of_bytes(self.zr, others - LEVELS + 1, self.z_sem.at[0, q]).wait()
            self.of_bytes(self.zr, LEVELS - 1, self.z_sem.at[1, q], True).wait()

        @pl.when(jnp.logical_not(self.last))
        def _():
            self.keep(q, self.zs, self.zr, self.own_sem.at[0, q]).wait()
            self.of_bytes(self.zr, others, self.z_sem.at[2, q]).wait()
            self.of_bytes(self.zr, others - LEVELS, self.z_sem.at[0, q]).wait()
            self.of_bytes(self.zr, LEVELS, self.z_sem.at[1, q], True).wait()

    def factor(self, wave_x, wave_y):
        inside = wave_x * wave_x + wave_y * wave_y < MX * MY
        weight = jnp.where(wave_x == 0, 1.0, 2.0) * jnp.where(wave_y == 0, 1.0, 2.0)
        return jnp.where(inside, weight, 0.0).astype(jnp.float32)

    def prepare(self):
        tiles = MX // LANES
        role = lax.rem(self.reg, self.roles)
        coupled = role < tiles
        first = jnp.where(coupled, role, 2 * (role - tiles))
        second = jnp.where(coupled, role, jnp.minimum(2 * (role - tiles) + 1, tiles - 1))
        block = LANES

        @pl.loop(0, self.waves.shape[1] // block)
        def _(n):
            rows = pl.ds(pl.multiple_of(n * block, block), block)
            lane = lax.broadcasted_iota(jnp.int32, (block, LANES), 1)
            wave_y = lax.broadcasted_iota(jnp.int32, (block, LANES), 0) + lax.rem(n * block, MY)
            waves = [2 * lax.rem(lane + tile * LANES, MX // 2) + self.lev for tile in (first, second)]
            kx_term = 2.0 * math.pi / NLON * waves[0].astype(jnp.float32)
            ky_term = 2.0 * math.pi / NLAT * wave_y.astype(jnp.float32)
            self.waves[0, rows] = kx_term * kx_term + ky_term * ky_term
            self.waves[1, rows] = self.factor(waves[0], wave_y)
            self.waves[2, rows] = self.factor(waves[1], wave_y)

    def solve(self, q):
        self.arrive(q)
        roles = self.roles
        tiles = MX // LANES
        role = lax.rem(self.reg, roles)
        coupled = role < tiles
        speed = self.speed[q * LEVELS + self.reg // roles]
        block = 2 * LANES
        gate = jnp.where(coupled, 1.0, 0.0)

        @pl.loop(0, self.lf.shape[0] // block)
        def _(n):
            rows = pl.ds(pl.multiple_of(n * block, block), block)
            spectral = jnp.dot(self.lf[rows], self.zr[q], preferred_element_type=jnp.float32) * (1.0 / NLAT)
            laplace = self.waves[0, rows]
            one, two = spectral[:, :LANES], spectral[:, LANES:]
            div_new = (one + laplace * two) / (1.0 + speed * laplace)
            pres_new = two - speed * div_new
            one = jnp.where(gate > 0.5, div_new, one) * self.waves[1, rows]
            two = jnp.where(gate > 0.5, pres_new, two) * self.waves[2, rows]
            self.solved[rows, :LANES] = one.astype(jnp.bfloat16)
            self.solved[rows, LANES:] = two.astype(jnp.bfloat16)

        @pl.loop(0, self.lb.shape[0] // block)
        def _(n):
            rows = pl.ds(pl.multiple_of(n * block, block), block)
            back = jnp.dot(self.lb[rows], self.solved[...], preferred_element_type=jnp.float32)
            self.bs[q % 2, rows] = back.astype(jnp.bfloat16)

        self.keep(q, self.bs, self.br, self.own_sem.at[1, q]).start()
        send_sem = self.b_sem.at[q]
        recv_sem = self.bg_sem.at[q, jnp.where(role < roles // 2, 0, 1), self.reg // roles]
        half_sem = self.bg_sem.at[q, 2, self.reg // roles]

        @pl.when(self.last)
        def _():
            for i in range(1, self.count):
                self.to_peer(q, self.bs, self.br, send_sem, half_sem, lax.bitwise_xor(self.reg, i), True).start()

        @pl.when(jnp.logical_not(self.last))
        def _():
            for i in range(1, self.count):
                self.to_peer(q, self.bs, self.br, send_sem, recv_sem, lax.bitwise_xor(self.reg, i)).start()

    def cross(self, q):
        roles = self.roles
        role = lax.rem(self.reg, roles)
        self.keep(q, self.bs, self.br, self.own_sem.at[1, q]).wait()
        sizes = (roles // 2, roles // 2 - 1, 1)
        inside = (role < roles // 2, (role >= roles // 2) & (role < roles - 1), self.last)
        for level in range(LEVELS):
            here = self.reg // roles == level
            for n, copy in enumerate(self.yb_copies(q, level)):
                half = n == 2
                own = here & inside[n]

                if sizes[n] > 1:
                    @pl.when(own)
                    def _():
                        self.of_bytes(self.br, sizes[n] - 1, self.bg_sem.at[q, n, level], half).wait()

                @pl.when(jnp.logical_not(own))
                def _():
                    self.of_bytes(self.br, sizes[n], self.bg_sem.at[q, n, level], half).wait()

                copy.start()

        @pl.when(self.last)
        def _():
            self.of_bytes(self.br, self.count - 1, self.b_sem.at[q], True).wait()

        @pl.when(jnp.logical_not(self.last))
        def _():
            self.of_bytes(self.br, self.count - 1, self.b_sem.at[q]).wait()

    def assemble(self, source, q, start, sign):
        for level in range(LEVELS):
            for field in range(FIELDS):
                place = pl.ds((level * FIELDS + field) * self.rows, self.rows)
                for tile, (role, half) in enumerate(self.places(field)):
                    rows = pl.ds((level * self.roles + role) * self.rows, self.rows)
                    piece = source[q, rows, half * LANES : (half + 1) * LANES]
                    piece = piece if sign is None else piece * sign
                    self.asm[place, start + tile * LANES : start + (tile + 1) * LANES] = piece

    def finish(self, q):
        self.assemble(self.br, q, 0, self.sign.astype(jnp.bfloat16))
        for level in range(LEVELS):
            for copy in self.yb_copies(q, level):
                copy.wait()
        self.assemble(self.yb, q, MX, None)

        @pl.when(q >= 1)
        def _():
            self.out_copy(q - 1).wait()

        block = 2 * LANES

        @pl.loop(0, self.cols // block)
        def _(n):
            cols = pl.ds(pl.multiple_of(n * block, block), block)
            value = jnp.dot(self.asm[...], self.tb[:, cols], preferred_element_type=jnp.float32)
            self.ost[:, :, cols] = value.astype(jnp.bfloat16).reshape(LEVELS * FIELDS, self.rows, block)

        self.out_copy(q).start()

    def run(self):
        barrier = pltpu.get_barrier_semaphore()

        @pl.loop(1, self.count)
        def _(i):
            peer = lax.rem(self.reg + i, self.count)
            pl.semaphore_signal(barrier, inc=1, device_id=(peer, self.lev), device_id_type=MESH)

        for near in (0, 1, self.count - 1):
            peer = lax.rem(self.reg + near, self.count)
            pl.semaphore_signal(barrier, inc=1, device_id=(peer, 1 - self.lev), device_id_type=MESH)

        for copy in self.loads(0):
            copy.start()
        total = self.chunks

        @pl.when(self.last)
        def _():
            self.zr[:, :, LANES:] = jnp.zeros_like(self.zr[:, :, LANES:])

        def at(step, offset, stage, *field):
            q = step - offset

            @pl.when((q >= 0) & (q < total))
            def _():
                stage(q, *field)

        self.prepare()
        self.loads(0, slice(1))[0].wait()
        self.pack(0)
        pl.semaphore_wait(barrier, self.count + 2)
        for copy in self.halos(0):
            copy.start()
        for copy in self.tables():
            copy.start()

        @pl.loop(0, total)
        def _(step):
            for copy in self.loads(step, slice(1, None)):
                copy.wait()
            self.decode()
            for copy in self.halos(step):
                copy.wait()
            self.unpack(step)
            for field in range(FIELDS):
                self.spread_taps(step, field)

                if field == FIELDS - 1:
                    @pl.when(step + 1 < total)
                    def _():
                        for copy in self.loads(step + 1):
                            copy.start()

                self.blend(step, field)

                if field == 0:
                    @pl.when(step == 0)
                    def _():
                        for copy in self.tables():
                            copy.wait()

                if field == FIELDS - 1:
                    @pl.when(step + 1 < total)
                    def _():
                        self.loads(step + 1, slice(1))[0].wait()
                        self.pack(step + 1)
                        for copy in self.halos(step + 1):
                            copy.start()

                self.leave(step, field)
                if field == 0:
                    at(step, 1, self.join, FIELDS - 1)
                else:
                    self.join(step, field - 1)

            at(step, 3, self.finish)
            at(step, 2, self.cross)

            @pl.when(step == total - 1)
            def _():
                self.join(step, FIELDS - 1)

            at(step, 1, self.solve)

        self.solve(total - 1)
        self.finish(total - 3)
        self.cross(total - 2)
        self.cross(total - 1)
        self.finish(total - 2)
        self.finish(total - 1)
        self.out_copy(total - 1).wait()


def step_kernel(*refs):
    Step(refs[:11], refs[11], refs[12:]).run()


def row_source(rows, level, field, row):
    k = level * FIELDS + field
    if row < 0:
        return LEVELS * rows + HALO * (k + 1) + row
    if row >= rows:
        return LEVELS * rows + 2 * ROWS + HALO * k + row - rows
    return level * rows + row


def paired_device(state_now, dep_cell, weight_code, wave_speed):
    stacked, rows, cols = state_now.shape
    levels = stacked // FIELDS
    chunks = levels // LEVELS
    count = lax.axis_size("reg")
    run = rows // SUB
    reach = run + 2 * HALO
    fields = LEVELS * FIELDS
    packed = 2 * ROWS
    perm = np.zeros((FIELDS, reach * ROWS, LEVELS * rows + 2 * packed), np.float32)
    pick = np.zeros((2, packed, fields * ROWS), np.float32)
    for k in range(fields):
        for near in range(HALO):
            pick[0, HALO * k + near, ROWS * k + ROWS - HALO + near] = 1.0
            pick[1, HALO * k + near, ROWS * k + near] = 1.0
    perm_codes = np.zeros((run * ROWS, LEVELS * rows), np.float32)
    for level in range(LEVELS):
        for sub in range(SUB):
            for near in range(reach):
                for field in range(FIELDS):
                    source = row_source(rows, level, field, run * sub + near - HALO)
                    perm[field, near * ROWS + level * SUB + sub, source] = 1.0
            for near in range(run):
                perm_codes[near * ROWS + level * SUB + sub, level * rows + run * sub + near] = 1.0
    half = MX // 2
    waves = [host_waves(NLON, 2 * np.arange(half) + odd, cols) for odd in range(2)]
    lon_fwd = np.stack(waves)
    lat = host_waves(NLAT, np.arange(MY), NLAT)
    order = (np.arange(NLAT).reshape(count, SUB, run).transpose(0, 2, 1)).reshape(-1)
    bf16 = jnp.bfloat16
    consts = [jnp.asarray(a, bf16) for a in (perm, perm_codes, pick)]
    consts += [jnp.asarray(np.ascontiguousarray(a)) for a in
               (lon_fwd, lon_fwd.transpose(0, 2, 1), lat[order].T, lat)]
    taps = 2 * HALO + 1
    vm, dma = pltpu.VMEM, pltpu.SemaphoreType.DMA
    scratch = [
        vm((fields, rows, cols + 2 * LANES), bf16),
        vm((chunks, 2, packed, cols + 2 * LANES), bf16),
        vm((chunks, rows, LANES), bf16),
        vm((2, 2, packed, cols), bf16),
        vm((2, rows, LANES), bf16),
        vm((2, 2, packed, LANES), bf16),
        vm((LEVELS, rows, cols), jnp.int32),
        vm((LEVELS, rows, cols), jnp.int32),
        vm((3, run, ROWS, cols), bf16),
        vm((taps, reach, ROWS, cols), bf16),
        vm((2, FIELDS, run * ROWS, cols), bf16),
        vm((2, FIELDS, LEVELS, rows, MX), bf16),
        vm((chunks, FIELDS, LEVELS, rows, MX), bf16),
        vm((2, NLAT, 2 * LANES), bf16),
        vm((chunks, NLAT, 2 * LANES), bf16),
        vm((3, 2 * MY, LANES), jnp.float32),
        vm((2 * MY, 2 * LANES), bf16),
        vm((2, NLAT, 2 * LANES), bf16),
        vm((chunks, NLAT, 2 * LANES), bf16),
        vm((chunks, NLAT, 2 * LANES), bf16),
        vm((fields * rows, 2 * MX), bf16),
        vm((fields, rows, cols), bf16),
        vm((2, cols, MX), bf16),
        vm((2 * MX, cols), bf16),
        vm((2 * MY, NLAT), bf16),
        vm((NLAT, 2 * MY), bf16),
        dma((3,)), dma((2, chunks, 7)), dma((6,)), dma((2, chunks, FIELDS)), dma((3, chunks)), dma((chunks,)), dma((chunks, 3, LEVELS)),
        dma((2, chunks, 3 * LEVELS)), dma((2, chunks)), dma((1,)),
    ]
    hbm = pl.BlockSpec(memory_space=pl.ANY)
    vmem = pl.BlockSpec(memory_space=pltpu.VMEM)
    return pl.pallas_call(
        step_kernel,
        out_shape=jax.ShapeDtypeStruct((stacked, rows, cols), bf16),
        in_specs=[hbm] * 3 + [pl.BlockSpec(memory_space=pltpu.SMEM)] + [vmem] * 3 + [hbm] * 4,
        out_specs=hbm,
        scratch_shapes=scratch,
        compiler_params=pltpu.CompilerParams(vmem_limit_bytes=60 << 20, collective_id=0, has_side_effects=True),
        cost_estimate=pl.CostEstimate(flops=20 * 10**9, bytes_accessed=40 * 10**6, transcendentals=0),
        name="step",
    )(state_now, dep_cell, weight_code, wave_speed, *consts)


def solution(mesh):
    placed = (P(None, "reg", "lev"), P(None, "reg", "lev"), P(None, "reg", "lev"), P())
    paired = mesh.shape["lev"] == 2 and mesh.shape["reg"] == 16
    return jax.shard_map(
        paired_device if paired else per_device,
        mesh=mesh,
        in_specs=placed,
        out_specs=P(None, "reg", "lev"),
        check_vma=False,
    )
```

```python
import math

import jax
import jax.numpy as jnp
import ml_dtypes
import numpy as np
from jax import lax
from jax.experimental import pallas as pl
from jax.experimental.pallas import tpu as pltpu
from jax.sharding import PartitionSpec as P

NLAT = 1280
NLON = 2560
MX = 640
MY = 640
FIELDS = 3
HALO = 4
LANES = 128
ROWS = 16


def padded_2(block, sides, width):
    for axis, dim in sides:
        count = lax.axis_size(axis)
        forward = [(i, i + 1) for i in range(count - 1)]
        forward.append((count - 1, 0))
        backward = [(target, source) for source, target in forward]
        low = lax.ppermute(
            lax.slice_in_dim(block, block.shape[dim] - width, None, axis=dim), axis, forward
        )
        high = lax.ppermute(lax.slice_in_dim(block, 0, width, axis=dim), axis, backward)
        block = jnp.concatenate([low, block, high], axis=dim)
    return block


def wave_table(length, modes, offset, amount):
    position = offset + lax.iota(jnp.int32, amount)
    wavenum = lax.iota(jnp.int32, 2 * modes) % modes
    product = position[:, None] * wavenum[None, :] % length
    angles = product.astype(jnp.float32) * (2.0 * math.pi / length)
    cosine_part = lax.iota(jnp.int32, 2 * modes) < modes
    return jnp.where(cosine_part[None, :], jnp.cos(angles), jnp.sin(angles)).astype(jnp.bfloat16)


def implicit_solve(spectral, xindex, speeds):
    wave_x = xindex % MX
    wave_y = lax.iota(jnp.int32, 2 * MY) % MY
    kx_term = 2.0 * math.pi / NLON * wave_x.astype(jnp.float32)
    ky_term = 2.0 * math.pi / NLAT * wave_y.astype(jnp.float32)
    laplace = kx_term[:, None] ** 2 + ky_term[None, :] ** 2
    inside = wave_x[:, None] * wave_x[:, None] + wave_y[None, :] * wave_y[None, :] < MX * MY
    weight_x = jnp.where(wave_x == 0, 1.0, 2.0)
    weight_y = jnp.where(wave_y == 0, 1.0, 2.0)
    factor = jnp.where(inside, weight_x[:, None] * weight_y[None, :], 0.0).astype(jnp.float32)
    speed_sq = speeds[:, None, None]
    vorticity = spectral[:, 0]
    divergence = spectral[:, 1]
    pressure = spectral[:, 2]
    div_new = (divergence + laplace * pressure) / (1.0 + speed_sq * laplace)
    pres_new = pressure - speed_sq * div_new
    stacked = jnp.stack([vorticity, div_new, pres_new], axis=1)
    return (stacked * factor[None, None]).astype(jnp.bfloat16)


def shift_weights(cell_code, code_index):
    shift_row = cell_code // (2 * HALO) - HALO
    shift_col = cell_code % (2 * HALO) - HALO
    weight_row = (code_index // 17).astype(jnp.float32) / 16.0
    weight_col = (code_index % 17).astype(jnp.float32) / 16.0
    row_weights = []
    col_weights = []
    for offset in range(-HALO, HALO + 1):
        row_weights.append(
            jnp.where(shift_row == offset, 1.0 - weight_row, 0.0)
            + jnp.where(shift_row + 1 == offset, weight_row, 0.0)
        )
        col_weights.append(
            jnp.where(shift_col == offset, 1.0 - weight_col, 0.0)
            + jnp.where(shift_col + 1 == offset, weight_col, 0.0)
        )
    return (row_weights, col_weights)


def interpolate_local(padded, row_weights, col_weights):
    levels, rows_pad, cols_pad = padded.shape
    rows_here = rows_pad - 2 * HALO
    cols_here = cols_pad - 2 * HALO
    blended = jnp.zeros((levels, rows_here, cols_here), jnp.float32)
    for row_step in range(2 * HALO + 1):
        inner = jnp.zeros((levels, rows_here, cols_here), jnp.float32)
        for col_step in range(2 * HALO + 1):
            window = padded[:, row_step : row_step + rows_here, col_step : col_step + cols_here]
            inner = inner + col_weights[col_step] * window.astype(jnp.float32)
        blended = blended + row_weights[row_step] * inner
    return blended.astype(jnp.bfloat16)


def per_device(state_now, dep_cell, weight_code, wave_speed):
    stacked, rows_here, cols_here = state_now.shape
    levels = stacked // FIELDS
    col_first = lax.axis_index("lev") * cols_here
    grouped = state_now.reshape(levels, FIELDS, rows_here, cols_here)
    row_weights, col_weights = shift_weights(dep_cell, weight_code)
    passes = []
    for which_field in range(FIELDS):
        padded = padded_2(grouped[:, which_field], (("reg", 1), ("lev", 2)), HALO)
        passes.append(interpolate_local(padded, row_weights, col_weights))
    upstream = jnp.stack(passes, axis=1).reshape(stacked, rows_here, cols_here)
    lon_table = wave_table(NLON, MX, 0, NLON)
    full_rows = lax.all_to_all(upstream, "lev", split_axis=0, concat_axis=2, tiled=True)
    lon_sum = jnp.einsum("krj,jc->krc", full_rows, lon_table, preferred_element_type=jnp.float32)
    lon_coef = (lon_sum / NLON).astype(jnp.bfloat16)
    lat_table = wave_table(NLAT, MY, 0, NLAT)
    spectral = (
        jnp.einsum(
            "klc,ly->kcy",
            lax.all_to_all(lon_coef, "reg", split_axis=2, concat_axis=1, tiled=True),
            lat_table,
            preferred_element_type=jnp.float32,
        )
        / NLAT
    )
    share = spectral.shape[1]
    xindex = lax.axis_index("reg") * share + lax.iota(jnp.int32, share)
    level_count = spectral.shape[0] // FIELDS
    speeds = lax.dynamic_slice_in_dim(
        wave_speed, lax.axis_index("lev") * level_count, level_count, 0
    )
    solved = implicit_solve(spectral.reshape(level_count, FIELDS, share, 2 * MY), xindex, speeds)
    solved = solved.reshape(level_count * FIELDS, share, 2 * MY)
    back_lat = jnp.einsum(
        "kcy,ly->kcl", solved, lat_table, preferred_element_type=jnp.float32
    ).astype(jnp.bfloat16)
    back_coef = lax.all_to_all(back_lat, "reg", split_axis=2, concat_axis=1, tiled=True)
    own_table = wave_table(NLON, MX, col_first, cols_here)
    return jnp.einsum(
        "kcr,jc->krj",
        lax.all_gather(back_coef, "lev", axis=0, tiled=True),
        own_table,
        preferred_element_type=jnp.float32,
    ).astype(jnp.bfloat16)


LEVELS = 2
SUB = 8
MESH = pl.DeviceIdType.MESH


def host_waves(length, wavenums, amount):
    angles = (np.arange(amount)[:, None] * wavenums[None, :] % length) * (2.0 * np.pi / length)
    both = np.concatenate([np.cos(angles), np.sin(angles)], axis=1)
    return both.astype(np.float32).astype(ml_dtypes.bfloat16)


def mux_pair(parts, bits):
    for bit, step in zip(bits, (4, 2, 1)):
        parts = [jnp.where(bit, parts[i + step], parts[i]) for i in range(len(parts) - step)]
    return parts


def bit_masks(cell):
    masks = []
    for bit in (32.0, 16.0, 8.0, 4.0, 2.0, 1.0):
        mask = cell >= jnp.asarray(bit, cell.dtype)
        masks.append(mask)
        cell = jnp.where(mask, cell - jnp.asarray(bit, cell.dtype), cell)
    return masks


class Step:
    def __init__(self, ins, out, scratch):
        (self.x, self.dep, self.weight, self.speed, self.perm, self.perm_codes, self.pick,
         self.lon_fwd, self.lon_back, self.lat_fwd, self.lat_back) = ins
        self.out = out
        (self.xbuf, self.hrow, self.hedge, self.srow, self.sedge, self.scorner, self.dbuf, self.wbuf, self.codes, self.parts, self.shift, self.up, self.yl, self.yr, self.zs, self.zr,
         self.waves, self.solved, self.bs, self.br, self.yb, self.asm, self.ost, self.tf, self.tb, self.lf, self.lb,
         self.load_sem, self.halo_sem, self.table_sem, self.y_sem, self.z_sem, self.b_sem, self.bg_sem, self.yb_sem, self.own_sem, self.out_sem) = scratch
        self.reg, self.lev = lax.axis_index("reg"), lax.axis_index("lev")
        self.count = lax.axis_size("reg")
        self.rows = self.x.shape[1]
        self.roles = self.count // LEVELS
        self.last = lax.rem(self.reg, self.roles) == self.roles - 1
        self.cols = self.x.shape[2]
        self.chunks = self.dep.shape[0] // LEVELS
        self.sign = (1 - 2 * self.lev).astype(jnp.float32)

    def loads(self, q, which=slice(None)):
        fields = LEVELS * FIELDS
        ks = pl.ds(q * fields, fields)
        vs = pl.ds(q * LEVELS, LEVELS)
        mid = pl.ds(LANES, self.cols)
        pairs = [
            (self.x.at[ks], self.xbuf.at[:, :, mid]),
            (self.dep.at[vs], self.dbuf),
            (self.weight.at[vs], self.wbuf),
        ]
        return [pltpu.make_async_copy(a, b, self.load_sem.at[i]) for i, (a, b) in list(enumerate(pairs))[which]]

    def halos(self, q):
        slot = q % 2
        up = lax.rem(self.reg + self.count - 1, self.count)
        down = lax.rem(self.reg + 1, self.count)
        other = 1 - self.lev
        mid = pl.ds(LANES, self.cols)
        left, right = pl.ds(0, LANES), pl.ds(LANES + self.cols, LANES)
        moves = [(self.sedge.at[slot], self.hedge.at[q], self.reg, other)]
        for side, to in enumerate((down, up)):
            moves.append((self.srow.at[slot, side], self.hrow.at[q, side, :, mid], to, self.lev))
            for lanes in (left, right):
                moves.append((self.scorner.at[slot, side], self.hrow.at[q, side, :, lanes], to, other))
        return [
            pltpu.make_async_remote_copy(
                src_ref=src, dst_ref=dst, send_sem=self.halo_sem.at[0, q, n], recv_sem=self.halo_sem.at[1, q, n],
                device_id=(reg, lev), device_id_type=MESH)
            for n, (src, dst, reg, lev) in enumerate(moves)
        ]

    def pack(self, q):
        slot = q % 2
        fields = LEVELS * FIELDS
        last = self.cols
        lane = lax.broadcasted_iota(jnp.int32, (1, LANES), 1)
        near = lane < LANES // 2
        edge = jnp.zeros((self.rows, LANES), jnp.float32)
        for k in range(fields):
            first = self.xbuf[k, :, LANES : 2 * LANES].astype(jnp.float32)
            final = self.xbuf[k, :, last : last + LANES].astype(jnp.float32)
            both = jnp.where(near, first, final)
            shift = 2 * HALO * k
            here = lax.rem(lane + (HALO + LANES - shift), LANES) < 2 * HALO
            edge = jnp.where(here, pltpu.roll(both, shift, axis=1) if shift else both, edge)
        self.sedge[slot] = edge.astype(jnp.bfloat16)
        for side, start in enumerate((self.rows - ROWS, 0)):
            slab = self.xbuf[:, start : start + ROWS, LANES : LANES + last].reshape(fields * ROWS, last)
            rows = jnp.dot(self.pick[side], slab, preferred_element_type=jnp.float32)
            self.srow[slot, side] = rows.astype(jnp.bfloat16)
            self.scorner[slot, side] = jnp.where(near, rows[:, :LANES], rows[:, last - LANES :]).astype(jnp.bfloat16)

    def unpack(self, q):
        edge = self.hedge[q].astype(jnp.float32)
        for k in range(LEVELS * FIELDS):
            tile = pltpu.roll(edge, LANES - 2 * HALO * k, axis=1) if k else edge
            tile = tile.astype(jnp.bfloat16)
            self.xbuf[k, :, :LANES] = tile
            self.xbuf[k, :, LANES + self.cols :] = tile

    def tables(self):
        other = 1 - self.lev
        pairs = [
            (self.lon_fwd.at[other], self.tf.at[1]), (self.lon_fwd.at[self.lev], self.tf.at[0]),
            (self.lat_fwd, self.lf), (self.lat_back, self.lb),
            (self.lon_back.at[self.lev], self.tb.at[pl.ds(0, MX)]), (self.lon_back.at[other], self.tb.at[pl.ds(MX, MX)]),
        ]
        return [pltpu.make_async_copy(a, b, self.table_sem.at[i]) for i, (a, b) in enumerate(pairs)]

    def y_copy(self, q, field):
        return pltpu.make_async_remote_copy(
            src_ref=self.yl.at[q % 2, field], dst_ref=self.yr.at[q, field],
            send_sem=self.y_sem.at[0, q, field], recv_sem=self.y_sem.at[1, q, field],
            device_id=(self.reg, 1 - self.lev), device_id_type=MESH)

    def yb_copies(self, q, level):
        full = self.count // LEVELS * self.rows
        near = (self.count // LEVELS // 2) * self.rows
        start = level * full
        parts = [
            (pl.ds(start, near), slice(None)),
            (pl.ds(start + near, full - near - self.rows), slice(None)),
            (pl.ds(start + full - self.rows, self.rows), pl.ds(0, LANES)),
        ]
        return [
            pltpu.make_async_remote_copy(
                src_ref=self.br.at[q, rows, lanes], dst_ref=self.yb.at[q, rows, lanes],
                send_sem=self.yb_sem.at[0, q, 3 * level + n], recv_sem=self.yb_sem.at[1, q, 3 * level + n],
                device_id=(self.reg, 1 - self.lev), device_id_type=MESH)
            for n, (rows, lanes) in enumerate(parts)
        ]

    def block(self, index):
        return pl.ds(pl.multiple_of(index * self.rows, ROWS), self.rows)

    def to_peer(self, q, src, dst, send, recv, peer, half=False):
        lanes = pl.ds(0, LANES) if half else slice(None)
        return pltpu.make_async_remote_copy(
            src_ref=src.at[q % 2, self.block(peer), lanes], dst_ref=dst.at[q, self.block(self.reg), lanes],
            send_sem=send, recv_sem=recv, device_id=(peer, self.lev), device_id_type=MESH)

    def of_bytes(self, ref, blocks, sem, half=False):
        lanes = pl.ds(0, LANES) if half else slice(None)
        part = ref.at[0, pl.ds(0, blocks * self.rows), lanes]
        return pltpu.make_async_copy(part, part, sem)

    def keep(self, q, src, dst, sem, half=False):
        lanes = pl.ds(0, LANES) if half else slice(None)
        return pltpu.make_async_copy(
            src.at[q % 2, self.block(self.reg), lanes], dst.at[q, self.block(self.reg), lanes], sem)

    def out_copy(self, q):
        fields = LEVELS * FIELDS
        return pltpu.make_async_copy(self.ost, self.out.at[pl.ds(q * fields, fields)], self.out_sem.at[0])

    def decode(self):
        rows = LEVELS * self.rows
        block = 2 * LANES

        @pl.loop(0, self.cols // block)
        def _(n):
            cols = pl.ds(pl.multiple_of(n * block, block), block)
            cell = self.dbuf[:, :, cols].reshape(rows, block)
            both = self.wbuf[:, :, cols].reshape(rows, block)
            high = (both * 241) >> 12
            for i, code in enumerate((cell, high, both - 17 * high)):
                code = code.astype(jnp.float32).astype(jnp.bfloat16)
                moved = jnp.dot(self.perm_codes[...], code, preferred_element_type=jnp.float32)
                shape = (self.rows // SUB, ROWS, block)
                if i:
                    self.parts[i - 1, :, :, cols] = (moved * (1.0 / 16.0)).reshape(shape)
                    continue
                for bit, mask in enumerate(bit_masks(moved.astype(jnp.bfloat16))):
                    flag = jnp.where(mask, jnp.asarray(1.0, jnp.bfloat16), jnp.asarray(0.0, jnp.bfloat16))
                    self.codes[bit, :, :, cols] = flag.reshape(shape)

    def spread_taps(self, q, field):
        width = self.cols
        taps = 2 * HALO + 1
        part = self.shift.shape[1] // 2

        @pl.loop(0, 2)
        def _(half):
            parts = [self.xbuf[field], self.xbuf[FIELDS + field], self.hrow[q, 0], self.hrow[q, 1]]
            block = jnp.concatenate(parts, axis=0)
            perm = self.perm[field, pl.ds(pl.multiple_of(half * part * ROWS, ROWS), part * ROWS)]
            moved = jnp.dot(perm, block, preferred_element_type=jnp.float32)
            for tap in range(taps):
                turned = pltpu.roll(moved, (HALO - tap) % moved.shape[1], axis=1)[:, LANES : LANES + width]
                self.shift[tap, pl.ds(half * part, part)] = turned.astype(jnp.bfloat16).reshape(part, ROWS, width)

    def blend(self, q, field):
        slot = q % 2
        taps = 2 * HALO + 1
        tile = 2 * LANES
        tiles = self.cols // tile

        @pl.loop(0, self.rows // SUB // 2 * tiles)
        def _(step):
            row = 2 * (step // tiles)
            cols = pl.ds(pl.multiple_of(step % tiles * tile, tile), tile)
            masks = [[self.codes[bit, row + sub, :, cols] > 0 for bit in range(6)] for sub in range(2)]
            near, far = [[], []], [[], []]
            for tap in range(taps):
                parts = [self.shift[tap, row + i, :, cols] for i in range(taps + 1)]
                for sub in range(2):
                    first, second = mux_pair(parts[sub : sub + taps], masks[sub][:3])
                    near[sub].append(first)
                    far[sub].append(second)
            for sub in range(2):
                low = [part.astype(jnp.float32) for part in mux_pair(near[sub], masks[sub][3:])]
                high = [part.astype(jnp.float32) for part in mux_pair(far[sub], masks[sub][3:])]
                weight_row = self.parts[0, row + sub, :, cols]
                weight_col = self.parts[1, row + sub, :, cols]
                upper = low[0] + weight_col * (low[1] - low[0])
                lower = high[0] + weight_col * (high[1] - high[0])
                value = upper + weight_row * (lower - upper)
                place = pl.ds(pl.multiple_of((row + sub) * ROWS, ROWS), ROWS)
                self.up[slot, field, place, cols] = value.astype(jnp.bfloat16)

    def partial(self, q, field, table):
        total = jnp.dot(self.up[q % 2, field], self.tf[table], preferred_element_type=jnp.float32) * (1.0 / NLON)
        total = total.reshape(self.rows // SUB, LEVELS, SUB, total.shape[1])
        return [total[:, level].reshape(self.rows, total.shape[3]) for level in range(LEVELS)]

    def leave(self, q, field):
        for level, part in enumerate(self.partial(q, field, 1)):
            self.yl[q % 2, field, level] = part.astype(jnp.bfloat16)
        self.y_copy(q, field).start()

    def places(self, field):
        tiles = MX // LANES
        if field > 0:
            return [(tile, field - 1) for tile in range(tiles)]
        return [(tiles + tile // 2, tile % 2) for tile in range(tiles)]

    def join(self, q, field):
        roles = self.roles
        tiles = MX // LANES
        self.y_copy(q, field).wait()
        for level, part in enumerate(self.partial(q, field, 0)):
            whole = (part * self.sign + self.yr[q, field, level].astype(jnp.float32)).astype(jnp.bfloat16)
            for tile, (role, half) in enumerate(self.places(field)):
                rows = pl.ds((level * roles + role) * self.rows, self.rows)
                piece = whole[:, tile * LANES : (tile + 1) * LANES]
                self.zs[q % 2, rows, half * LANES : (half + 1) * LANES] = piece
        if field == 1:
            return
        full_sem, half_sem, recv_sem = self.z_sem.at[0, q], self.z_sem.at[1, q], self.z_sem.at[2, q]
        spread = roles - tiles if field == 0 else tiles
        for other in range(LEVELS):
            level = lax.rem(self.reg // roles + other, LEVELS)
            for turn in range(spread):
                role = tiles + turn if field == 0 else lax.rem(self.reg + turn, tiles)
                half = field == 0 and turn == spread - 1
                peer = level * roles + role
                send_sem = half_sem if half else full_sem

                @pl.when(peer != self.reg)
                def _():
                    self.to_peer(q, self.zs, self.zr, send_sem, recv_sem, peer, half).start()

                @pl.when(peer == self.reg)
                def _():
                    self.keep(q, self.zs, self.zr, self.own_sem.at[0, q], half).start()

    def arrive(self, q):
        others = self.count - 1

        @pl.when(self.last)
        def _():
            self.keep(q, self.zs, self.zr, self.own_sem.at[0, q], True).wait()
            self.of_bytes(self.zr, others, self.z_sem.at[2, q], True).wait()
            self.of_bytes(self.zr, others - LEVELS + 1, self.z_sem.at[0, q]).wait()
            self.of_bytes(self.zr, LEVELS - 1, self.z_sem.at[1, q], True).wait()

        @pl.when(jnp.logical_not(self.last))
        def _():
            self.keep(q, self.zs, self.zr, self.own_sem.at[0, q]).wait()
            self.of_bytes(self.zr, others, self.z_sem.at[2, q]).wait()
            self.of_bytes(self.zr, others - LEVELS, self.z_sem.at[0, q]).wait()
            self.of_bytes(self.zr, LEVELS, self.z_sem.at[1, q], True).wait()

    def factor(self, wave_x, wave_y):
        inside = wave_x * wave_x + wave_y * wave_y < MX * MY
        weight = jnp.where(wave_x == 0, 1.0, 2.0) * jnp.where(wave_y == 0, 1.0, 2.0)
        return jnp.where(inside, weight, 0.0).astype(jnp.float32)

    def prepare(self):
        tiles = MX // LANES
        role = lax.rem(self.reg, self.roles)
        coupled = role < tiles
        first = jnp.where(coupled, role, 2 * (role - tiles))
        second = jnp.where(coupled, role, jnp.minimum(2 * (role - tiles) + 1, tiles - 1))
        block = LANES

        @pl.loop(0, self.waves.shape[1] // block)
        def _(n):
            rows = pl.ds(pl.multiple_of(n * block, block), block)
            lane = lax.broadcasted_iota(jnp.int32, (block, LANES), 1)
            wave_y = lax.broadcasted_iota(jnp.int32, (block, LANES), 0) + lax.rem(n * block, MY)
            waves = [2 * lax.rem(lane + tile * LANES, MX // 2) + self.lev for tile in (first, second)]
            kx_term = 2.0 * math.pi / NLON * waves[0].astype(jnp.float32)
            ky_term = 2.0 * math.pi / NLAT * wave_y.astype(jnp.float32)
            self.waves[0, rows] = kx_term * kx_term + ky_term * ky_term
            self.waves[1, rows] = self.factor(waves[0], wave_y)
            self.waves[2, rows] = self.factor(waves[1], wave_y)

    def solve(self, q):
        self.arrive(q)
        roles = self.roles
        tiles = MX // LANES
        role = lax.rem(self.reg, roles)
        coupled = role < tiles
        speed = self.speed[q * LEVELS + self.reg // roles]
        block = 2 * LANES
        gate = jnp.where(coupled, 1.0, 0.0)

        @pl.loop(0, self.lf.shape[0] // block)
        def _(n):
            rows = pl.ds(pl.multiple_of(n * block, block), block)
            spectral = jnp.dot(self.lf[rows], self.zr[q], preferred_element_type=jnp.float32) * (1.0 / NLAT)
            laplace = self.waves[0, rows]
            one, two = spectral[:, :LANES], spectral[:, LANES:]
            div_new = (one + laplace * two) / (1.0 + speed * laplace)
            pres_new = two - speed * div_new
            one = jnp.where(gate > 0.5, div_new, one) * self.waves[1, rows]
            two = jnp.where(gate > 0.5, pres_new, two) * self.waves[2, rows]
            self.solved[rows, :LANES] = one.astype(jnp.bfloat16)
            self.solved[rows, LANES:] = two.astype(jnp.bfloat16)

        @pl.loop(0, self.lb.shape[0] // block)
        def _(n):
            rows = pl.ds(pl.multiple_of(n * block, block), block)
            back = jnp.dot(self.lb[rows], self.solved[...], preferred_element_type=jnp.float32)
            self.bs[q % 2, rows] = back.astype(jnp.bfloat16)

        self.keep(q, self.bs, self.br, self.own_sem.at[1, q]).start()
        send_sem = self.b_sem.at[q]
        recv_sem = self.bg_sem.at[q, jnp.where(role < roles // 2, 0, 1), self.reg // roles]
        half_sem = self.bg_sem.at[q, 2, self.reg // roles]

        @pl.when(self.last)
        def _():
            for i in range(1, self.count):
                self.to_peer(q, self.bs, self.br, send_sem, half_sem, lax.bitwise_xor(self.reg, i), True).start()

        @pl.when(jnp.logical_not(self.last))
        def _():
            for i in range(1, self.count):
                self.to_peer(q, self.bs, self.br, send_sem, recv_sem, lax.bitwise_xor(self.reg, i)).start()

    def cross(self, q):
        roles = self.roles
        role = lax.rem(self.reg, roles)
        self.keep(q, self.bs, self.br, self.own_sem.at[1, q]).wait()
        sizes = (roles // 2, roles // 2 - 1, 1)
        inside = (role < roles // 2, (role >= roles // 2) & (role < roles - 1), self.last)
        for level in range(LEVELS):
            here = self.reg // roles == level
            for n, copy in enumerate(self.yb_copies(q, level)):
                half = n == 2
                own = here & inside[n]

                if sizes[n] > 1:
                    @pl.when(own)
                    def _():
                        self.of_bytes(self.br, sizes[n] - 1, self.bg_sem.at[q, n, level], half).wait()

                @pl.when(jnp.logical_not(own))
                def _():
                    self.of_bytes(self.br, sizes[n], self.bg_sem.at[q, n, level], half).wait()

                copy.start()

        @pl.when(self.last)
        def _():
            self.of_bytes(self.br, self.count - 1, self.b_sem.at[q], True).wait()

        @pl.when(jnp.logical_not(self.last))
        def _():
            self.of_bytes(self.br, self.count - 1, self.b_sem.at[q]).wait()

    def assemble(self, source, q, start, sign):
        for level in range(LEVELS):
            for field in range(FIELDS):
                place = pl.ds((level * FIELDS + field) * self.rows, self.rows)
                for tile, (role, half) in enumerate(self.places(field)):
                    rows = pl.ds((level * self.roles + role) * self.rows, self.rows)
                    piece = source[q, rows, half * LANES : (half + 1) * LANES]
                    piece = piece if sign is None else piece * sign
                    self.asm[place, start + tile * LANES : start + (tile + 1) * LANES] = piece

    def finish(self, q):
        self.assemble(self.br, q, 0, self.sign.astype(jnp.bfloat16))
        for level in range(LEVELS):
            for copy in self.yb_copies(q, level):
                copy.wait()
        self.assemble(self.yb, q, MX, None)

        @pl.when(q >= 1)
        def _():
            self.out_copy(q - 1).wait()

        block = 2 * LANES

        @pl.loop(0, self.cols // block)
        def _(n):
            cols = pl.ds(pl.multiple_of(n * block, block), block)
            value = jnp.dot(self.asm[...], self.tb[:, cols], preferred_element_type=jnp.float32)
            self.ost[:, :, cols] = value.astype(jnp.bfloat16).reshape(LEVELS * FIELDS, self.rows, block)

        self.out_copy(q).start()

    def run(self):
        barrier = pltpu.get_barrier_semaphore()

        @pl.loop(1, self.count)
        def _(i):
            peer = lax.rem(self.reg + i, self.count)
            pl.semaphore_signal(barrier, inc=1, device_id=(peer, self.lev), device_id_type=MESH)

        for near in (0, 1, self.count - 1):
            peer = lax.rem(self.reg + near, self.count)
            pl.semaphore_signal(barrier, inc=1, device_id=(peer, 1 - self.lev), device_id_type=MESH)

        for copy in self.loads(0):
            copy.start()
        total = self.chunks

        def at(step, offset, stage, *field):
            q = step - offset

            @pl.when((q >= 0) & (q < total))
            def _():
                stage(q, *field)

        self.loads(0, slice(1))[0].wait()
        self.pack(0)
        pl.semaphore_wait(barrier, self.count + 2)
        for copy in self.halos(0):
            copy.start()
        for copy in self.tables():
            copy.start()

        @pl.when(self.last)
        def _():
            self.zr[:, :, LANES:] = jnp.zeros_like(self.zr[:, :, LANES:])

        self.prepare()

        @pl.loop(0, total)
        def _(step):
            for copy in self.loads(step, slice(1, None)):
                copy.wait()
            self.decode()
            for copy in self.halos(step):
                copy.wait()
            self.unpack(step)
            for field in range(FIELDS):
                self.spread_taps(step, field)

                if field == FIELDS - 1:
                    @pl.when(step + 1 < total)
                    def _():
                        for copy in self.loads(step + 1):
                            copy.start()

                self.blend(step, field)

                if field == 0:
                    @pl.when(step == 0)
                    def _():
                        for copy in self.tables():
                            copy.wait()

                if field == FIELDS - 1:
                    @pl.when(step + 1 < total)
                    def _():
                        self.loads(step + 1, slice(1))[0].wait()
                        self.pack(step + 1)
                        for copy in self.halos(step + 1):
                            copy.start()

                self.leave(step, field)
                if field == 0:
                    at(step, 1, self.join, FIELDS - 1)
                else:
                    self.join(step, field - 1)

            at(step, 2, self.cross)
            at(step, 3, self.finish)

            @pl.when(step == total - 1)
            def _():
                self.join(step, FIELDS - 1)

            at(step, 1, self.solve)

        self.finish(total - 3)
        self.solve(total - 1)
        self.cross(total - 2)
        self.cross(total - 1)
        self.finish(total - 2)
        self.finish(total - 1)
        self.out_copy(total - 1).wait()


def step_kernel(*refs):
    Step(refs[:11], refs[11], refs[12:]).run()


def row_source(rows, level, field, row):
    k = level * FIELDS + field
    if row < 0:
        return LEVELS * rows + HALO * (k + 1) + row
    if row >= rows:
        return LEVELS * rows + 2 * ROWS + HALO * k + row - rows
    return level * rows + row


def paired_device(state_now, dep_cell, weight_code, wave_speed):
    stacked, rows, cols = state_now.shape
    levels = stacked // FIELDS
    chunks = levels // LEVELS
    count = lax.axis_size("reg")
    run = rows // SUB
    reach = run + 2 * HALO
    fields = LEVELS * FIELDS
    packed = 2 * ROWS
    perm = np.zeros((FIELDS, reach * ROWS, LEVELS * rows + 2 * packed), np.float32)
    pick = np.zeros((2, packed, fields * ROWS), np.float32)
    for k in range(fields):
        for near in range(HALO):
            pick[0, HALO * k + near, ROWS * k + ROWS - HALO + near] = 1.0
            pick[1, HALO * k + near, ROWS * k + near] = 1.0
    perm_codes = np.zeros((run * ROWS, LEVELS * rows), np.float32)
    for level in range(LEVELS):
        for sub in range(SUB):
            for near in range(reach):
                for field in range(FIELDS):
                    source = row_source(rows, level, field, run * sub + near - HALO)
                    perm[field, near * ROWS + level * SUB + sub, source] = 1.0
            for near in range(run):
                perm_codes[near * ROWS + level * SUB + sub, level * rows + run * sub + near] = 1.0
    half = MX // 2
    waves = [host_waves(NLON, 2 * np.arange(half) + odd, cols) for odd in range(2)]
    lon_fwd = np.stack(waves)
    lat = host_waves(NLAT, np.arange(MY), NLAT)
    order = (np.arange(NLAT).reshape(count, SUB, run).transpose(0, 2, 1)).reshape(-1)
    bf16 = jnp.bfloat16
    consts = [jnp.asarray(a, bf16) for a in (perm, perm_codes, pick)]
    consts += [jnp.asarray(np.ascontiguousarray(a)) for a in
               (lon_fwd, lon_fwd.transpose(0, 2, 1), lat[order].T, lat)]
    taps = 2 * HALO + 1
    vm, dma = pltpu.VMEM, pltpu.SemaphoreType.DMA
    scratch = [
        vm((fields, rows, cols + 2 * LANES), bf16),
        vm((chunks, 2, packed, cols + 2 * LANES), bf16),
        vm((chunks, rows, LANES), bf16),
        vm((2, 2, packed, cols), bf16),
        vm((2, rows, LANES), bf16),
        vm((2, 2, packed, LANES), bf16),
        vm((LEVELS, rows, cols), jnp.int32),
        vm((LEVELS, rows, cols), jnp.int32),
        vm((6, run, ROWS, cols), bf16),
        vm((2, run, ROWS, cols), jnp.float32),
        vm((taps, reach, ROWS, cols), bf16),
        vm((2, FIELDS, run * ROWS, cols), bf16),
        vm((2, FIELDS, LEVELS, rows, MX), bf16),
        vm((chunks, FIELDS, LEVELS, rows, MX), bf16),
        vm((2, NLAT, 2 * LANES), bf16),
        vm((chunks, NLAT, 2 * LANES), bf16),
        vm((3, 2 * MY, LANES), jnp.float32),
        vm((2 * MY, 2 * LANES), bf16),
        vm((2, NLAT, 2 * LANES), bf16),
        vm((chunks, NLAT, 2 * LANES), bf16),
        vm((chunks, NLAT, 2 * LANES), bf16),
        vm((fields * rows, 2 * MX), bf16),
        vm((fields, rows, cols), bf16),
        vm((2, cols, MX), bf16),
        vm((2 * MX, cols), bf16),
        vm((2 * MY, NLAT), bf16),
        vm((NLAT, 2 * MY), bf16),
        dma((3,)), dma((2, chunks, 7)), dma((6,)), dma((2, chunks, FIELDS)), dma((3, chunks)), dma((chunks,)), dma((chunks, 3, LEVELS)),
        dma((2, chunks, 3 * LEVELS)), dma((2, chunks)), dma((1,)),
    ]
    hbm = pl.BlockSpec(memory_space=pl.ANY)
    vmem = pl.BlockSpec(memory_space=pltpu.VMEM)
    return pl.pallas_call(
        step_kernel,
        out_shape=jax.ShapeDtypeStruct((stacked, rows, cols), bf16),
        in_specs=[hbm] * 3 + [pl.BlockSpec(memory_space=pltpu.SMEM)] + [vmem] * 3 + [hbm] * 4,
        out_specs=hbm,
        scratch_shapes=scratch,
        compiler_params=pltpu.CompilerParams(vmem_limit_bytes=60 << 20, collective_id=0, has_side_effects=True),
        cost_estimate=pl.CostEstimate(flops=20 * 10**9, bytes_accessed=40 * 10**6, transcendentals=0),
        name="step",
    )(state_now, dep_cell, weight_code, wave_speed, *consts)


def solution(mesh):
    placed = (P(None, "reg", "lev"), P(None, "reg", "lev"), P(None, "reg", "lev"), P())
    paired = mesh.shape["lev"] == 2 and mesh.shape["reg"] == 16
    return jax.shard_map(
        paired_device if paired else per_device,
        mesh=mesh,
        in_specs=placed,
        out_specs=P(None, "reg", "lev"),
        check_vma=False,
    )
```
